512 devices in a mesh: tile: 64 (over x, z_lo, core), tm: 8 (over z_hi, y).
Axes of the slice: x: 4, y: 4, z: 16 (z_hi: 2, z_lo: 8; z = z_hi * 8 + z_lo), core: 2. Of those that a mesh axis runs over, the one named last changes fastest.
Arguments:
- controls: float32 [16, 512, 8, 512], P('tm', 'tile'), may hold values from -6 to 6
- perturbations: bfloat16 [8, 16, 4, 512, 8, 512], P('tm', None, None, 'tile'), may hold values from -6 to 6
- owner: int32 [16], replicated, may hold values from 0 to 15, each once
- land_mask: int32 [512, 512], P('tile'), may hold values 0 or 1
- diffusivity: float32 [2, 8], replicated, may hold values from 0.2 to 0.24
Outputs:
- increment: float32 [8, 4, 512, 8, 512], P('tm', None, 'tile')
The draws below stay inside these ranges and needn't reach their ends.
Inputs may be any that keep to these rules, and one draw needn't show every extreme that they name: owner names every member exactly once.
All inputs are finite; a program needn't handle non-finite values. No bound on the sum of `land_mask` on one device may be relied on, other than what follows from the above.
Results may differ from the reference program's by a relative error of at most 0.0029.
Values may be sent and summed in bfloat16 or wider, within the bound.
A program may use at most 64 MiB of HBM per device.

```python
import math
import jax
import jax.numpy as jnp
from jax import lax

NY = 512
LEV = 8
VARS = 4
SWEEPS = 4
MEMBERS = 16
TIMES = 8
NX = 512


def draw_controls(key, part):
    sign_key = jax.random.fold_in(key, 11)
    noise_key = jax.random.fold_in(key, 12)
    member_sign = 1.0 - 2.0 * jax.random.randint(sign_key, (MEMBERS,), 0, 2).astype(jnp.float32)
    row_sign = 1.0 - 2.0 * (jnp.arange(NX, dtype=jnp.int32) % 2).astype(jnp.float32)
    noise = jax.random.normal(noise_key, (MEMBERS, NX, LEV, NY), jnp.float32)
    field = 5.5 * member_sign[:, None, None, None] * row_sign[None, :, None, None] + 0.3 * noise
    return jnp.clip(field, -6.0, 6.0).astype(jnp.float32)


def place_ends(values, stream_key, least, largest):
    longest = values.shape.index(max(values.shape))
    spots = []
    for shift in (0, 1):
        where = [jax.random.randint(jax.random.fold_in(stream_key, axis), (), 0, length) for axis, length in enumerate(values.shape)]
        where[longest] = (where[longest] + shift) % values.shape[longest]
        spots.append(tuple(where))
    return values.at[spots[0]].set(least).at[spots[1]].set(largest)


def level_of(rng, dims, cuts, smallest, largest):
    factor_of, own = 1.0, jax.random.fold_in(rng, 6)
    for position, parts in cuts:
        heights = jnp.exp(jax.random.uniform(jax.random.fold_in(own, position), (parts,), jnp.float32, smallest / len(cuts), largest / len(cuts)))
        factor_of = factor_of * jnp.repeat(heights, dims[position] // parts).reshape([-1 if axis == position else 1 for axis in range(len(dims))])
    return factor_of


def bell_draw(stream_key, shape, scale, most, shards=(), held_as=jnp.bfloat16):
    gain = level_of(stream_key, shape, shards, -0.22, 0.18) if shards else 1.0
    values = jax.random.normal(stream_key, shape, jnp.float32) * scale * gain
    return jnp.minimum(jnp.maximum(values, -most), most).astype(held_as)


def setup_inputs(seed: int = 0) -> dict:
    arg_keys = jax.random.split(jax.random.key(seed), 6)
    controls = draw_controls(jax.random.fold_in(arg_keys[5], 71), 0)
    perturbations = bell_draw(arg_keys[1], (TIMES, MEMBERS, VARS, NX, LEV, NY), 1.0, 6.0, ((0, 8), (3, 64)))
    owner = jax.random.permutation(arg_keys[2], MEMBERS).astype(jnp.int32)
    land_mask = place_ends((jax.random.randint(arg_keys[3], (NX, NY), 0, 5) < 2).astype(jnp.int32), jax.random.fold_in(arg_keys[3], 1), 0, 1)
    diffusivity = jnp.clip(jnp.exp(jax.random.uniform(arg_keys[4], (2, LEV), jnp.float32, math.log(0.2), math.log(0.24))), 0.2, 0.24)
    return dict(controls=controls, perturbations=perturbations, owner=owner, land_mask=land_mask, diffusivity=diffusivity)


def weight_sweep(field, coef):
    padded = jnp.pad(field, ((0, 0), (1, 1), (0, 0), (1, 1)))
    coef_pad = jnp.pad(coef, ((1, 1), (0, 0), (1, 1)))
    flux = 0.5 * (coef + coef_pad[:-2, :, 1:-1]) * (padded[:, :-2, :, 1:-1] - field)
    flux = flux + 0.5 * (coef + coef_pad[2:, :, 1:-1]) * (padded[:, 2:, :, 1:-1] - field)
    flux = flux + 0.5 * (coef + coef_pad[1:-1, :, :-2]) * (padded[:, 1:-1, :, :-2] - field)
    flux = flux + 0.5 * (coef + coef_pad[1:-1, :, 2:]) * (padded[:, 1:-1, :, 2:] - field)
    return field + flux

def reference(controls, perturbations, owner, land_mask, diffusivity):
    diffuse_coef = jnp.where(land_mask[:, None, :] == 1, diffusivity[1][None, :, None], diffusivity[0][None, :, None])
    smooth = controls
    for sweep_index in range(SWEEPS):
        smooth = weight_sweep(smooth, diffuse_coef)
    weights = smooth.astype(jnp.bfloat16)
    by_member = jnp.zeros_like(weights).at[owner].set(weights)
    factor = 1.0 / math.sqrt(MEMBERS - 1)

    def one_time(pert_time):
        summed = jnp.zeros(pert_time.shape[1:], jnp.float32)
        for member in range(MEMBERS):
            summed = summed + pert_time[member].astype(jnp.float32) * by_member[member].astype(jnp.float32)[None]
        return summed * factor
    return lax.map(one_time, perturbations)
```

```python
import math

import jax
import jax.numpy as jnp
from jax import lax
from jax.sharding import PartitionSpec as P

SWEEPS = 4


def halo_rows(cells, width, dim):
    count = lax.axis_size("tile")
    ends = count - 1
    head = lax.slice_in_dim(cells, 0, width, axis=dim)
    tail = lax.slice_in_dim(cells, cells.shape[dim] - width, cells.shape[dim], axis=dim)
    before = lax.ppermute(tail, "tile", [(i, i + 1) for i in range(ends)])
    after = lax.ppermute(head, "tile", [(i + 1, i) for i in range(ends)])
    return jnp.concatenate([before, cells, after], axis=dim)


def weight_sweep(field, coef):
    padded = jnp.pad(field, ((0, 0), (1, 1), (0, 0), (1, 1)))
    coef_pad = jnp.pad(coef, ((1, 1), (0, 0), (1, 1)))
    flux = 0.5 * (coef + coef_pad[:-2, :, 1:-1]) * (padded[:, :-2, :, 1:-1] - field)
    flux = flux + 0.5 * (coef + coef_pad[2:, :, 1:-1]) * (padded[:, 2:, :, 1:-1] - field)
    flux = flux + 0.5 * (coef + coef_pad[1:-1, :, :-2]) * (padded[:, 1:-1, :, :-2] - field)
    flux = flux + 0.5 * (coef + coef_pad[1:-1, :, 2:]) * (padded[:, 1:-1, :, 2:] - field)
    return field + flux


def on_device(controls, perturbations, owner, land_mask, diffusivity):
    rows = controls.shape[1]
    width = SWEEPS
    tile = lax.axis_index("tile")
    count = lax.axis_size("tile")
    grow = tile * rows - width + jnp.arange(rows + 2 * width)
    inside = (grow >= 0) & (grow < count * rows)

    mask_wide = halo_rows(land_mask, width, 0)
    coef = jnp.where(
        mask_wide[:, None, :] == 1, diffusivity[1][None, :, None], diffusivity[0][None, :, None]
    )
    coef = jnp.where(inside[:, None, None], coef, 0.0)
    keep = inside[None, :, None, None]
    smooth = jnp.where(keep, halo_rows(controls, width, 1), 0.0)
    for sweep_index in range(SWEEPS):
        smooth = jnp.where(keep, weight_sweep(smooth, coef), 0.0)
    weights = smooth[:, width:width + rows].astype(jnp.bfloat16)

    every = lax.all_gather(weights, "tm", axis=0, tiled=True)
    by_member = jnp.zeros_like(every).at[owner].set(every)
    member_count = owner.shape[0]
    factor = 1.0 / math.sqrt(member_count - 1)
    summed = jnp.einsum(
        "mvxly,mxly->vxly", perturbations[0], by_member, preferred_element_type=jnp.float32
    )
    return (summed * factor)[None]


def solution(mesh):
    return jax.shard_map(
        on_device,
        mesh=mesh,
        in_specs=(
            P("tm", "tile", None, None),
            P("tm", None, None, "tile", None, None),
            P(),
            P("tile", None),
            P(),
        ),
        out_specs=P("tm", None, "tile", None, None),
        check_vma=False,
    )
```

```python
import functools
import math

import jax
import jax.numpy as jnp
from jax import lax
from jax.experimental import pallas as pl
from jax.experimental.pallas import tpu as pltpu
from jax.sharding import PartitionSpec as P

MESH = pl.DeviceIdType.MESH

SWEEPS = 4


def halo_rows(cells, width, dim):
    count = lax.axis_size("tile")
    ends = count - 1
    head = lax.slice_in_dim(cells, 0, width, axis=dim)
    tail = lax.slice_in_dim(cells, cells.shape[dim] - width, cells.shape[dim], axis=dim)
    before = lax.ppermute(tail, "tile", [(i, i + 1) for i in range(ends)])
    after = lax.ppermute(head, "tile", [(i + 1, i) for i in range(ends)])
    return jnp.concatenate([before, cells, after], axis=dim)


def weight_sweep(field, coef):
    padded = jnp.pad(field, ((0, 0), (1, 1), (0, 0), (1, 1)))
    coef_pad = jnp.pad(coef, ((1, 1), (0, 0), (1, 1)))
    flux = 0.5 * (coef + coef_pad[:-2, :, 1:-1]) * (padded[:, :-2, :, 1:-1] - field)
    flux = flux + 0.5 * (coef + coef_pad[2:, :, 1:-1]) * (padded[:, 2:, :, 1:-1] - field)
    flux = flux + 0.5 * (coef + coef_pad[1:-1, :, :-2]) * (padded[:, 1:-1, :, :-2] - field)
    flux = flux + 0.5 * (coef + coef_pad[1:-1, :, 2:]) * (padded[:, 1:-1, :, 2:] - field)
    return field + flux


def gather_kernel(half, w_ref, out_ref, send_sem, recv_sem):
    tile = lax.axis_index("tile")
    me = lax.axis_index("tm")
    groups = lax.axis_size("tm")
    depth = w_ref.shape[0]
    zp = lax.rem(me + half, groups)
    base = me - lax.rem(me, half)
    peers = [base + lax.rem(lax.rem(me, half) + d, half) for d in range(1, half)]

    barrier = pltpu.get_barrier_semaphore()
    for dev in [zp] + peers:
        pl.semaphore_signal(barrier, inc=1, device_id=(tile, dev), device_id_type=MESH)
    pl.semaphore_wait(barrier, half)

    def block(g):
        return out_ref.at[pl.ds(g * depth, depth)]

    def copy(src, g, dev, slot):
        return pltpu.make_async_remote_copy(
            src_ref=src, dst_ref=block(g), send_sem=send_sem.at[slot],
            recv_sem=recv_sem.at[g], device_id=(tile, dev), device_id_type=MESH,
        )

    sends = [copy(w_ref, me, zp, 0)]
    sends[0].start()
    for i, p in enumerate(peers):
        c = copy(w_ref, me, p, 1 + i)
        c.start()
        sends.append(c)
    block(me)[...] = w_ref[...]
    copy(w_ref, zp, zp, 0).wait_recv()
    for i, p in enumerate(peers):
        c = copy(block(zp), zp, p, half + i)
        c.start()
        sends.append(c)
    for p in peers:
        copy(w_ref, p, p, 0).wait_recv()
        copy(w_ref, lax.rem(p + half, groups), p, 0).wait_recv()
    for c in sends:
        c.wait_send()


def gather_weights(weights):
    groups = lax.axis_size("tm")
    half = 4 if groups % 4 == 0 else groups // 2
    depth = weights.shape[0]
    return pl.pallas_call(
        functools.partial(gather_kernel, half),
        out_shape=jax.ShapeDtypeStruct((groups * depth,) + weights.shape[1:], weights.dtype),
        in_specs=[pl.BlockSpec(memory_space=pltpu.VMEM)],
        out_specs=pl.BlockSpec(memory_space=pltpu.VMEM),
        scratch_shapes=[
            pltpu.SemaphoreType.DMA((2 * half,)),
            pltpu.SemaphoreType.DMA((groups,)),
        ],
        compiler_params=pltpu.CompilerParams(collective_id=0, has_side_effects=True),
    )(weights)


def on_device(controls, perturbations, owner, land_mask, diffusivity):
    rows = controls.shape[1]
    width = SWEEPS
    tile = lax.axis_index("tile")
    count = lax.axis_size("tile")
    grow = tile * rows - width + jnp.arange(rows + 2 * width)
    inside = (grow >= 0) & (grow < count * rows)

    mask_wide = halo_rows(land_mask, width, 0)
    coef = jnp.where(
        mask_wide[:, None, :] == 1, diffusivity[1][None, :, None], diffusivity[0][None, :, None]
    )
    coef = jnp.where(inside[:, None, None], coef, 0.0)
    keep = inside[None, :, None, None]
    smooth = jnp.where(keep, halo_rows(controls, width, 1), 0.0)
    for sweep_index in range(SWEEPS):
        smooth = jnp.where(keep, weight_sweep(smooth, coef), 0.0)
    weights = smooth[:, width:width + rows].astype(jnp.bfloat16)

    every = gather_weights(weights)
    by_member = jnp.zeros_like(every).at[owner].set(every)
    member_count = owner.shape[0]
    factor = 1.0 / math.sqrt(member_count - 1)
    summed = jnp.einsum(
        "mvxly,mxly->vxly", perturbations[0], by_member, preferred_element_type=jnp.float32
    )
    return (summed * factor)[None]


def solution(mesh):
    return jax.shard_map(
        on_device,
        mesh=mesh,
        in_specs=(
            P("tm", "tile", None, None),
            P("tm", None, None, "tile", None, None),
            P(),
            P("tile", None),
            P(),
        ),
        out_specs=P("tm", None, "tile", None, None),
        check_vma=False,
    )
```

```python
import functools
import math

import jax
import jax.numpy as jnp
from jax import lax
from jax.experimental import pallas as pl
from jax.experimental.pallas import tpu as pltpu
from jax.sharding import PartitionSpec as P

MESH = pl.DeviceIdType.MESH

SWEEPS = 4


def weight_sweep(field, coef):
    padded = jnp.pad(field, ((0, 0), (1, 1), (0, 0), (1, 1)))
    coef_pad = jnp.pad(coef, ((1, 1), (0, 0), (1, 1)))
    flux = 0.5 * (coef + coef_pad[:-2, :, 1:-1]) * (padded[:, :-2, :, 1:-1] - field)
    flux = flux + 0.5 * (coef + coef_pad[2:, :, 1:-1]) * (padded[:, 2:, :, 1:-1] - field)
    flux = flux + 0.5 * (coef + coef_pad[1:-1, :, :-2]) * (padded[:, 1:-1, :, :-2] - field)
    flux = flux + 0.5 * (coef + coef_pad[1:-1, :, 2:]) * (padded[:, 1:-1, :, 2:] - field)
    return field + flux


def gather_kernel(half, w_ref, out_ref, send_sem, recv_sem):
    tile = lax.axis_index("tile")
    me = lax.axis_index("tm")
    groups = lax.axis_size("tm")
    depth = w_ref.shape[0]
    zp = lax.rem(me + half, groups)
    base = me - lax.rem(me, half)
    peers = [base + lax.rem(lax.rem(me, half) + d, half) for d in range(1, half)]

    barrier = pltpu.get_barrier_semaphore()
    for dev in [zp] + peers:
        pl.semaphore_signal(barrier, inc=1, device_id=(tile, dev), device_id_type=MESH)
    pl.semaphore_wait(barrier, half)

    def block(g):
        return out_ref.at[pl.ds(g * depth, depth)]

    def copy(src, g, dev, slot):
        return pltpu.make_async_remote_copy(
            src_ref=src, dst_ref=block(g), send_sem=send_sem.at[slot],
            recv_sem=recv_sem.at[g], device_id=(tile, dev), device_id_type=MESH,
        )

    sends = [copy(w_ref, me, zp, 0)]
    sends[0].start()
    for i, p in enumerate(peers):
        c = copy(w_ref, me, p, 1 + i)
        c.start()
        sends.append(c)
    block(me)[...] = w_ref[...]
    copy(w_ref, zp, zp, 0).wait_recv()
    for i, p in enumerate(peers):
        c = copy(block(zp), zp, p, half + i)
        c.start()
        sends.append(c)
    for p in peers:
        copy(w_ref, p, p, 0).wait_recv()
        copy(w_ref, lax.rem(p + half, groups), p, 0).wait_recv()
    for c in sends:
        c.wait_send()


def gather_weights(weights):
    groups = lax.axis_size("tm")
    half = 4 if groups % 4 == 0 else groups // 2
    depth = weights.shape[0]
    return pl.pallas_call(
        functools.partial(gather_kernel, half),
        out_shape=jax.ShapeDtypeStruct((groups * depth,) + weights.shape[1:], weights.dtype),
        in_specs=[pl.BlockSpec(memory_space=pltpu.VMEM)],
        out_specs=pl.BlockSpec(memory_space=pltpu.VMEM),
        scratch_shapes=[
            pltpu.SemaphoreType.DMA((2 * half,)),
            pltpu.SemaphoreType.DMA((groups,)),
        ],
        compiler_params=pltpu.CompilerParams(collective_id=0, has_side_effects=True),
    )(weights)


def halo_kernel(width, ctrl_ref, mask_ref, cb_ref, ca_ref, mb_ref, ma_ref, send_sem, recv_sem):
    me = lax.axis_index("tile")
    count = lax.axis_size("tile")
    tm = lax.axis_index("tm")
    rows = mask_ref.shape[0]
    right = lax.rem(me + 1, count)
    left = lax.rem(me + count - 1, count)

    barrier = pltpu.get_barrier_semaphore()
    for dev in (left, right):
        pl.semaphore_signal(barrier, inc=1, device_id=(dev, tm), device_id_type=MESH)
    pl.semaphore_wait(barrier, 2)

    head, tail = pl.ds(0, width), pl.ds(rows - width, width)
    plan = [
        (ctrl_ref.at[:, tail], cb_ref, right),
        (mask_ref.at[tail], mb_ref, right),
        (ctrl_ref.at[:, head], ca_ref, left),
        (mask_ref.at[head], ma_ref, left),
    ]
    copies = []
    for i, (src, dst, dev) in enumerate(plan):
        c = pltpu.make_async_remote_copy(
            src_ref=src, dst_ref=dst, send_sem=send_sem.at[i], recv_sem=recv_sem.at[i],
            device_id=(dev, tm), device_id_type=MESH,
        )
        c.start()
        copies.append(c)
    for c in copies:
        c.wait_send()
    for c in copies:
        c.wait_recv()


def exchange_halo(controls, land_mask, width):
    slots, _, lev, ny = controls.shape
    vmem = pl.BlockSpec(memory_space=pltpu.VMEM)
    ctrl = jax.ShapeDtypeStruct((slots, width, lev, ny), controls.dtype)
    mask = jax.ShapeDtypeStruct((width, ny), land_mask.dtype)
    return pl.pallas_call(
        functools.partial(halo_kernel, width),
        out_shape=(ctrl, ctrl, mask, mask),
        in_specs=[vmem, vmem],
        out_specs=(vmem, vmem, vmem, vmem),
        scratch_shapes=[pltpu.SemaphoreType.DMA((4,)), pltpu.SemaphoreType.DMA((4,))],
        compiler_params=pltpu.CompilerParams(collective_id=1, has_side_effects=True),
    )(controls, land_mask)


def on_device(controls, perturbations, owner, land_mask, diffusivity):
    rows = controls.shape[1]
    width = SWEEPS
    tile = lax.axis_index("tile")
    count = lax.axis_size("tile")
    grow = tile * rows - width + jnp.arange(rows + 2 * width)
    inside = (grow >= 0) & (grow < count * rows)

    cb, ca, mb, ma = exchange_halo(controls, land_mask, width)
    mask_wide = jnp.concatenate([mb, land_mask, ma], axis=0)
    coef = jnp.where(
        mask_wide[:, None, :] == 1, diffusivity[1][None, :, None], diffusivity[0][None, :, None]
    )
    coef = jnp.where(inside[:, None, None], coef, 0.0)
    keep = inside[None, :, None, None]
    smooth = jnp.where(keep, jnp.concatenate([cb, controls, ca], axis=1), 0.0)
    for sweep_index in range(SWEEPS):
        smooth = jnp.where(keep, weight_sweep(smooth, coef), 0.0)
    weights = smooth[:, width:width + rows].astype(jnp.bfloat16)

    every = gather_weights(weights)
    by_member = jnp.zeros_like(every).at[owner].set(every)
    member_count = owner.shape[0]
    factor = 1.0 / math.sqrt(member_count - 1)
    summed = jnp.einsum(
        "mvxly,mxly->vxly", perturbations[0], by_member, preferred_element_type=jnp.float32
    )
    return (summed * factor)[None]


def solution(mesh):
    return jax.shard_map(
        on_device,
        mesh=mesh,
        in_specs=(
            P("tm", "tile", None, None),
            P("tm", None, None, "tile", None, None),
            P(),
            P("tile", None),
            P(),
        ),
        out_specs=P("tm", None, "tile", None, None),
        check_vma=False,
    )
```

```python
import functools
import math

import jax
import jax.numpy as jnp
from jax import lax
from jax.experimental import pallas as pl
from jax.experimental.pallas import tpu as pltpu
from jax.sharding import PartitionSpec as P

MESH = pl.DeviceIdType.MESH

SWEEPS = 4


def weight_sweep(field, coef):
    padded = jnp.pad(field, ((0, 0), (1, 1), (0, 0), (1, 1)))
    coef_pad = jnp.pad(coef, ((1, 1), (0, 0), (1, 1)))
    flux = 0.5 * (coef + coef_pad[:-2, :, 1:-1]) * (padded[:, :-2, :, 1:-1] - field)
    flux = flux + 0.5 * (coef + coef_pad[2:, :, 1:-1]) * (padded[:, 2:, :, 1:-1] - field)
    flux = flux + 0.5 * (coef + coef_pad[1:-1, :, :-2]) * (padded[:, 1:-1, :, :-2] - field)
    flux = flux + 0.5 * (coef + coef_pad[1:-1, :, 2:]) * (padded[:, 1:-1, :, 2:] - field)
    return field + flux


def gather_sum_kernel(half, factor, owner_ref, w_ref, pert_ref, out_ref, held, send_sem, recv_sem):
    tile = lax.axis_index("tile")
    me = lax.axis_index("tm")
    groups = lax.axis_size("tm")
    depth = w_ref.shape[0]
    zp = lax.rem(me + half, groups)
    base = me - lax.rem(me, half)
    peers = [base + lax.rem(lax.rem(me, half) + d, half) for d in range(1, half)]

    barrier = pltpu.get_barrier_semaphore()
    for dev in [zp] + peers:
        pl.semaphore_signal(barrier, inc=1, device_id=(tile, dev), device_id_type=MESH)
    pl.semaphore_wait(barrier, half)

    def block(g):
        return held.at[pl.ds(g * depth, depth)]

    def copy(src, g, dev, slot):
        return pltpu.make_async_remote_copy(
            src_ref=src, dst_ref=block(g), send_sem=send_sem.at[slot],
            recv_sem=recv_sem.at[g], device_id=(tile, dev), device_id_type=MESH,
        )

    def add(src, g):
        for k in range(depth):
            member = owner_ref[g * depth + k]
            out_ref[...] += pert_ref[member].astype(jnp.float32) * src[k].astype(jnp.float32)[None]

    sends = [copy(w_ref, me, zp, 0)]
    sends[0].start()
    for i, p in enumerate(peers):
        c = copy(w_ref, me, p, 1 + i)
        c.start()
        sends.append(c)
    out_ref[...] = jnp.zeros(out_ref.shape, out_ref.dtype)
    add(w_ref, me)
    copy(w_ref, zp, zp, 0).wait_recv()
    for i, p in enumerate(peers):
        c = copy(block(zp), zp, p, half + i)
        c.start()
        sends.append(c)
    add(block(zp), zp)
    for p in peers:
        copy(w_ref, p, p, 0).wait_recv()
        add(block(p), p)
        far = lax.rem(p + half, groups)
        copy(w_ref, far, p, 0).wait_recv()
        add(block(far), far)
    for c in sends:
        c.wait_send()
    out_ref[...] = out_ref[...] * factor


def gather_and_sum(owner, weights, pert):
    groups = lax.axis_size("tm")
    half = 4 if groups % 4 == 0 else groups // 2
    depth = weights.shape[0]
    factor = 1.0 / math.sqrt(owner.shape[0] - 1)
    vmem = pl.BlockSpec(memory_space=pltpu.VMEM)
    return pl.pallas_call(
        functools.partial(gather_sum_kernel, half, factor),
        out_shape=jax.ShapeDtypeStruct(pert.shape[1:], jnp.float32),
        in_specs=[pl.BlockSpec(memory_space=pltpu.SMEM), vmem, vmem],
        out_specs=vmem,
        scratch_shapes=[
            pltpu.VMEM((groups * depth,) + weights.shape[1:], weights.dtype),
            pltpu.SemaphoreType.DMA((2 * half,)),
            pltpu.SemaphoreType.DMA((groups,)),
        ],
        compiler_params=pltpu.CompilerParams(
            collective_id=0, has_side_effects=True, vmem_limit_bytes=48 * 1024 * 1024
        ),
    )(owner, weights, pert)

def halo_kernel(width, ctrl_ref, mask_ref, cb_ref, ca_ref, mb_ref, ma_ref, send_sem, recv_sem):
    me = lax.axis_index("tile")
    count = lax.axis_size("tile")
    tm = lax.axis_index("tm")
    rows = mask_ref.shape[0]
    right = lax.rem(me + 1, count)
    left = lax.rem(me + count - 1, count)

    barrier = pltpu.get_barrier_semaphore()
    for dev in (left, right):
        pl.semaphore_signal(barrier, inc=1, device_id=(dev, tm), device_id_type=MESH)
    pl.semaphore_wait(barrier, 2)

    head, tail = pl.ds(0, width), pl.ds(rows - width, width)
    plan = [
        (ctrl_ref.at[:, tail], cb_ref, right),
        (mask_ref.at[tail], mb_ref, right),
        (ctrl_ref.at[:, head], ca_ref, left),
        (mask_ref.at[head], ma_ref, left),
    ]
    copies = []
    for i, (src, dst, dev) in enumerate(plan):
        c = pltpu.make_async_remote_copy(
            src_ref=src, dst_ref=dst, send_sem=send_sem.at[i], recv_sem=recv_sem.at[i],
            device_id=(dev, tm), device_id_type=MESH,
        )
        c.start()
        copies.append(c)
    for c in copies:
        c.wait_send()
    for c in copies:
        c.wait_recv()


def exchange_halo(controls, land_mask, width):
    slots, _, lev, ny = controls.shape
    vmem = pl.BlockSpec(memory_space=pltpu.VMEM)
    ctrl = jax.ShapeDtypeStruct((slots, width, lev, ny), controls.dtype)
    mask = jax.ShapeDtypeStruct((width, ny), land_mask.dtype)
    return pl.pallas_call(
        functools.partial(halo_kernel, width),
        out_shape=(ctrl, ctrl, mask, mask),
        in_specs=[vmem, vmem],
        out_specs=(vmem, vmem, vmem, vmem),
        scratch_shapes=[pltpu.SemaphoreType.DMA((4,)), pltpu.SemaphoreType.DMA((4,))],
        compiler_params=pltpu.CompilerParams(collective_id=1, has_side_effects=True),
    )(controls, land_mask)


def on_device(controls, perturbations, owner, land_mask, diffusivity):
    rows = controls.shape[1]
    width = SWEEPS
    tile = lax.axis_index("tile")
    count = lax.axis_size("tile")
    grow = tile * rows - width + jnp.arange(rows + 2 * width)
    inside = (grow >= 0) & (grow < count * rows)

    cb, ca, mb, ma = exchange_halo(controls, land_mask, width)
    mask_wide = jnp.concatenate([mb, land_mask, ma], axis=0)
    coef = jnp.where(
        mask_wide[:, None, :] == 1, diffusivity[1][None, :, None], diffusivity[0][None, :, None]
    )
    coef = jnp.where(inside[:, None, None], coef, 0.0)
    keep = inside[None, :, None, None]
    smooth = jnp.where(keep, jnp.concatenate([cb, controls, ca], axis=1), 0.0)
    for sweep_index in range(SWEEPS):
        smooth = jnp.where(keep, weight_sweep(smooth, coef), 0.0)
    weights = smooth[:, width:width + rows].astype(jnp.bfloat16)

    return gather_and_sum(owner, weights, perturbations[0])[None]


def solution(mesh):
    return jax.shard_map(
        on_device,
        mesh=mesh,
        in_specs=(
            P("tm", "tile", None, None),
            P("tm", None, None, "tile", None, None),
            P(),
            P("tile", None),
            P(),
        ),
        out_specs=P("tm", None, "tile", None, None),
        check_vma=False,
    )
```

```python
import functools
import math

import jax
import jax.numpy as jnp
from jax import lax
from jax.experimental import pallas as pl
from jax.experimental.pallas import tpu as pltpu
from jax.sharding import PartitionSpec as P

MESH = pl.DeviceIdType.MESH

SWEEPS = 4


def lane_shifts(u):
    ny = u.shape[-1]
    lane = lax.broadcasted_iota(jnp.int32, u.shape, u.ndim - 1)
    fwd, back = pltpu.roll(u, 1, u.ndim - 1), pltpu.roll(u, ny - 1, u.ndim - 1)
    rolled = pltpu.roll(lane, 1, u.ndim - 1)
    moved = (rolled == lane - 1) | (rolled == lane + ny - 1)
    lower = jnp.where(moved, fwd, back)
    upper = jnp.where(moved, back, fwd)
    zero = jnp.zeros_like(u)
    return jnp.where(lane == 0, zero, lower), jnp.where(lane == ny - 1, zero, upper)


def row_shifts(u):
    zero = jnp.zeros_like(u[:1])
    return jnp.concatenate([zero, u[:-1]], axis=0), jnp.concatenate([u[1:], zero], axis=0)


def fused_kernel(half, width, factor, owner_ref, diff_ref, ctrl_ref, mask_ref, pert_hbm,
                 out_ref, ext, mext, held, pert, send_sem, recv_sem, pert_sem):
    tile = lax.axis_index("tile")
    count = lax.axis_size("tile")
    me = lax.axis_index("tm")
    groups = lax.axis_size("tm")
    depth, rows, lev, ny = ctrl_ref.shape
    wide = rows + 2 * width
    right = lax.rem(tile + 1, count)
    left = lax.rem(tile + count - 1, count)
    zp = lax.rem(me + half, groups)
    base = me - lax.rem(me, half)
    peers = [base + lax.rem(lax.rem(me, half) + d, half) for d in range(1, half)]

    load = pltpu.make_async_copy(pert_hbm, pert, pert_sem.at[0])
    load.start()

    barrier = pltpu.get_barrier_semaphore()
    for dev in ((left, me), (right, me), (tile, zp)) + tuple((tile, p) for p in peers):
        pl.semaphore_signal(barrier, inc=1, device_id=dev, device_id_type=MESH)
    pl.semaphore_wait(barrier, 2 + half)

    head, tail = pl.ds(0, width), pl.ds(rows - width, width)
    plan = [
        (ctrl_ref.at[:, tail], ext.at[:, pl.ds(0, width)], right),
        (mask_ref.at[tail], mext.at[pl.ds(0, width)], right),
        (ctrl_ref.at[:, head], ext.at[:, pl.ds(width + rows, width)], left),
        (mask_ref.at[head], mext.at[pl.ds(width + rows, width)], left),
    ]
    halo = []
    for i, (src, dst, dev) in enumerate(plan):
        c = pltpu.make_async_remote_copy(
            src_ref=src, dst_ref=dst, send_sem=send_sem.at[i], recv_sem=recv_sem.at[i],
            device_id=(dev, me), device_id_type=MESH,
        )
        c.start()
        halo.append(c)
    ext[:, pl.ds(width, rows)] = ctrl_ref[...]
    mext[pl.ds(width, rows)] = mask_ref[...]
    for c in halo:
        c.wait_recv()

    grow = tile * rows - width + lax.broadcasted_iota(jnp.int32, (wide, lev, ny), 0)
    inside = (grow >= 0) & (grow < count * rows)
    levels = lax.broadcasted_iota(jnp.int32, (wide, lev, ny), 1)
    sea = jnp.zeros((wide, lev, ny), jnp.float32)
    land = jnp.zeros((wide, lev, ny), jnp.float32)
    for l in range(lev):
        sea = jnp.where(levels == l, diff_ref[0, l], sea)
        land = jnp.where(levels == l, diff_ref[1, l], land)
    landed = jnp.broadcast_to(mext[...][:, None, :], (wide, lev, ny)) == 1
    coef = jnp.where(inside, jnp.where(landed, land, sea), 0.0)
    cxm, cxp = row_shifts(coef)
    cym, cyp = lane_shifts(coef)
    axm, axp = 0.5 * (coef + cxm), 0.5 * (coef + cxp)
    aym, ayp = 0.5 * (coef + cym), 0.5 * (coef + cyp)

    def block(g):
        return held.at[pl.ds(g * depth, depth)]

    for k in range(depth):
        u = jnp.where(inside, ext[k], 0.0)
        for sweep_index in range(SWEEPS):
            uxm, uxp = row_shifts(u)
            uym, uyp = lane_shifts(u)
            flux = axm * (uxm - u)
            flux = flux + axp * (uxp - u)
            flux = flux + aym * (uym - u)
            flux = flux + ayp * (uyp - u)
            u = jnp.where(inside, u + flux, 0.0)
        held[me * depth + k] = u[width:width + rows].astype(held.dtype)

    for c in halo:
        c.wait_send()

    def copy(src, g, dev, slot):
        return pltpu.make_async_remote_copy(
            src_ref=src, dst_ref=block(g), send_sem=send_sem.at[4 + slot],
            recv_sem=recv_sem.at[4 + g], device_id=(tile, dev), device_id_type=MESH,
        )

    def add(src, g):
        for k in range(depth):
            member = owner_ref[g * depth + k]
            out_ref[...] += pert[member].astype(jnp.float32) * src[k].astype(jnp.float32)[None]

    sends = []
    for i, p in enumerate([zp] + peers):
        c = copy(block(me), me, p, i)
        c.start()
        sends.append(c)
    out_ref[...] = jnp.zeros(out_ref.shape, out_ref.dtype)
    load.wait()
    add(block(me), me)
    copy(block(zp), zp, zp, 0).wait_recv()
    for i, p in enumerate(peers):
        c = copy(block(zp), zp, p, half + i)
        c.start()
        sends.append(c)
    add(block(zp), zp)
    for p in peers:
        copy(block(p), p, p, 0).wait_recv()
        add(block(p), p)
        far = lax.rem(p + half, groups)
        copy(block(far), far, p, 0).wait_recv()
        add(block(far), far)
    for c in sends:
        c.wait_send()
    out_ref[...] = out_ref[...] * factor


def on_device(controls, perturbations, owner, land_mask, diffusivity):
    groups = lax.axis_size("tm")
    half = 4 if groups % 4 == 0 else groups // 2
    depth, rows, lev, ny = controls.shape
    width = SWEEPS
    pert = perturbations[0]
    factor = 1.0 / math.sqrt(owner.shape[0] - 1)
    vmem = pl.BlockSpec(memory_space=pltpu.VMEM)
    smem = pl.BlockSpec(memory_space=pltpu.SMEM)
    out = pl.pallas_call(
        functools.partial(fused_kernel, half, width, factor),
        out_shape=jax.ShapeDtypeStruct(pert.shape[1:], jnp.float32),
        in_specs=[smem, smem, vmem, vmem, pl.BlockSpec(memory_space=pl.ANY)],
        out_specs=vmem,
        scratch_shapes=[
            pltpu.VMEM((depth, rows + 2 * width, lev, ny), controls.dtype),
            pltpu.VMEM((rows + 2 * width, ny), land_mask.dtype),
            pltpu.VMEM((groups * depth, rows, lev, ny), jnp.bfloat16),
            pltpu.VMEM(pert.shape, pert.dtype),
            pltpu.SemaphoreType.DMA((4 + 2 * half,)),
            pltpu.SemaphoreType.DMA((4 + groups,)),
            pltpu.SemaphoreType.DMA((1,)),
        ],
        compiler_params=pltpu.CompilerParams(
            collective_id=0, has_side_effects=True, vmem_limit_bytes=48 * 1024 * 1024
        ),
    )(owner, diffusivity, controls, land_mask, pert)
    return out[None]


def solution(mesh):
    return jax.shard_map(
        on_device,
        mesh=mesh,
        in_specs=(
            P("tm", "tile", None, None),
            P("tm", None, None, "tile", None, None),
            P(),
            P("tile", None),
            P(),
        ),
        out_specs=P("tm", None, "tile", None, None),
        check_vma=False,
    )
```

```python
import functools
import math

import jax
import jax.numpy as jnp
from jax import lax
from jax.experimental import pallas as pl
from jax.experimental.pallas import tpu as pltpu
from jax.sharding import PartitionSpec as P

MESH = pl.DeviceIdType.MESH

SWEEPS = 4


def lane_shifts(u):
    ny = u.shape[-1]
    lane = lax.broadcasted_iota(jnp.int32, u.shape, u.ndim - 1)
    fwd, back = pltpu.roll(u, 1, u.ndim - 1), pltpu.roll(u, ny - 1, u.ndim - 1)
    rolled = pltpu.roll(lane, 1, u.ndim - 1)
    moved = (rolled == lane - 1) | (rolled == lane + ny - 1)
    lower = jnp.where(moved, fwd, back)
    upper = jnp.where(moved, back, fwd)
    zero = jnp.zeros_like(u)
    return jnp.where(lane == 0, zero, lower), jnp.where(lane == ny - 1, zero, upper)


def row_shifts(u):
    zero = jnp.zeros_like(u[:1])
    return jnp.concatenate([zero, u[:-1]], axis=0), jnp.concatenate([u[1:], zero], axis=0)


def fused_kernel(half, width, factor, owner_hbm, diff_hbm, ctrl_hbm, mask_hbm, pert_hbm,
                 out_ref, owner_ref, diff_ref, ctrl_ref, mask_ref, ext, mext, held, pert,
                 send_sem, recv_sem, load_sem):
    tile = lax.axis_index("tile")
    count = lax.axis_size("tile")
    me = lax.axis_index("tm")
    groups = lax.axis_size("tm")
    depth, rows, lev, ny = ctrl_hbm.shape
    wide = rows + 2 * width
    right = lax.rem(tile + 1, count)
    left = lax.rem(tile + count - 1, count)
    zp = lax.rem(me + half, groups)
    base = me - lax.rem(me, half)
    peers = [base + lax.rem(lax.rem(me, half) + d, half) for d in range(1, half)]

    loads = [
        pltpu.make_async_copy(src, dst, load_sem.at[i])
        for i, (src, dst) in enumerate(
            [(ctrl_hbm, ctrl_ref), (mask_hbm, mask_ref), (diff_hbm, diff_ref),
             (owner_hbm, owner_ref), (pert_hbm, pert)]
        )
    ]
    for c in loads:
        c.start()
    for c in loads[:4]:
        c.wait()

    barrier = pltpu.get_barrier_semaphore()
    for dev in ((left, me), (right, me), (tile, zp)) + tuple((tile, p) for p in peers):
        pl.semaphore_signal(barrier, inc=1, device_id=dev, device_id_type=MESH)
    pl.semaphore_wait(barrier, 2 + half)

    head, tail = pl.ds(0, width), pl.ds(rows - width, width)
    plan = [
        (ctrl_ref.at[:, tail], ext.at[:, pl.ds(0, width)], right),
        (mask_ref.at[tail], mext.at[pl.ds(0, width)], right),
        (ctrl_ref.at[:, head], ext.at[:, pl.ds(width + rows, width)], left),
        (mask_ref.at[head], mext.at[pl.ds(width + rows, width)], left),
    ]
    halo = []
    for i, (src, dst, dev) in enumerate(plan):
        c = pltpu.make_async_remote_copy(
            src_ref=src, dst_ref=dst, send_sem=send_sem.at[i], recv_sem=recv_sem.at[i],
            device_id=(dev, me), device_id_type=MESH,
        )
        c.start()
        halo.append(c)
    ext[:, pl.ds(width, rows)] = ctrl_ref[...]
    mext[pl.ds(width, rows)] = mask_ref[...]
    for c in halo:
        c.wait_recv()

    grow = tile * rows - width + lax.broadcasted_iota(jnp.int32, (wide, lev, ny), 0)
    inside = (grow >= 0) & (grow < count * rows)
    levels = lax.broadcasted_iota(jnp.int32, (wide, lev, ny), 1)
    sea = jnp.zeros((wide, lev, ny), jnp.float32)
    land = jnp.zeros((wide, lev, ny), jnp.float32)
    for l in range(lev):
        sea = jnp.where(levels == l, diff_ref[0, l], sea)
        land = jnp.where(levels == l, diff_ref[1, l], land)
    landed = jnp.broadcast_to(mext[...][:, None, :], (wide, lev, ny)) == 1
    coef = jnp.where(inside, jnp.where(landed, land, sea), 0.0)
    cxm, cxp = row_shifts(coef)
    cym, cyp = lane_shifts(coef)
    axm, axp = 0.5 * (coef + cxm), 0.5 * (coef + cxp)
    aym, ayp = 0.5 * (coef + cym), 0.5 * (coef + cyp)

    def block(g):
        return held.at[pl.ds(g * depth, depth)]

    for k in range(depth):
        u = jnp.where(inside, ext[k], 0.0)
        for sweep_index in range(SWEEPS):
            uxm, uxp = row_shifts(u)
            uym, uyp = lane_shifts(u)
            flux = axm * (uxm - u)
            flux = flux + axp * (uxp - u)
            flux = flux + aym * (uym - u)
            flux = flux + ayp * (uyp - u)
            u = jnp.where(inside, u + flux, 0.0)
        held[me * depth + k] = u[width:width + rows].astype(held.dtype)

    for c in halo:
        c.wait_send()

    def copy(src, g, dev, slot):
        return pltpu.make_async_remote_copy(
            src_ref=src, dst_ref=block(g), send_sem=send_sem.at[4 + slot],
            recv_sem=recv_sem.at[4 + g], device_id=(tile, dev), device_id_type=MESH,
        )

    def add(src, g):
        for k in range(depth):
            member = owner_ref[g * depth + k]
            out_ref[...] += pert[member].astype(jnp.float32) * src[k].astype(jnp.float32)[None]

    sends = []
    for i, p in enumerate([zp] + peers):
        c = copy(block(me), me, p, i)
        c.start()
        sends.append(c)
    out_ref[...] = jnp.zeros(out_ref.shape, out_ref.dtype)
    loads[4].wait()
    add(block(me), me)
    copy(block(zp), zp, zp, 0).wait_recv()
    for i, p in enumerate(peers):
        c = copy(block(zp), zp, p, half + i)
        c.start()
        sends.append(c)
    add(block(zp), zp)
    for p in peers:
        copy(block(p), p, p, 0).wait_recv()
        add(block(p), p)
        far = lax.rem(p + half, groups)
        copy(block(far), far, p, 0).wait_recv()
        add(block(far), far)
    for c in sends:
        c.wait_send()
    out_ref[...] = out_ref[...] * factor


def on_device(controls, perturbations, owner, land_mask, diffusivity):
    groups = lax.axis_size("tm")
    half = 4 if groups % 4 == 0 else groups // 2
    depth, rows, lev, ny = controls.shape
    width = SWEEPS
    pert = perturbations[0]
    factor = 1.0 / math.sqrt(owner.shape[0] - 1)
    vmem = pl.BlockSpec(memory_space=pltpu.VMEM)
    hbm = pl.BlockSpec(memory_space=pl.ANY)
    out = pl.pallas_call(
        functools.partial(fused_kernel, half, width, factor),
        out_shape=jax.ShapeDtypeStruct(pert.shape[1:], jnp.float32),
        in_specs=[hbm] * 5,
        out_specs=vmem,
        scratch_shapes=[
            pltpu.SMEM(owner.shape, owner.dtype),
            pltpu.SMEM(diffusivity.shape, diffusivity.dtype),
            pltpu.VMEM(controls.shape, controls.dtype),
            pltpu.VMEM(land_mask.shape, land_mask.dtype),
            pltpu.VMEM((depth, rows + 2 * width, lev, ny), controls.dtype),
            pltpu.VMEM((rows + 2 * width, ny), land_mask.dtype),
            pltpu.VMEM((groups * depth, rows, lev, ny), jnp.bfloat16),
            pltpu.VMEM(pert.shape, pert.dtype),
            pltpu.SemaphoreType.DMA((4 + 2 * half,)),
            pltpu.SemaphoreType.DMA((4 + groups,)),
            pltpu.SemaphoreType.DMA((5,)),
        ],
        compiler_params=pltpu.CompilerParams(
            collective_id=0, has_side_effects=True, vmem_limit_bytes=64 * 1024 * 1024
        ),
    )(owner, diffusivity, controls, land_mask, pert)
    return out[None]


def solution(mesh):
    return jax.shard_map(
        on_device,
        mesh=mesh,
        in_specs=(
            P("tm", "tile", None, None),
            P("tm", None, None, "tile", None, None),
            P(),
            P("tile", None),
            P(),
        ),
        out_specs=P("tm", None, "tile", None, None),
        check_vma=False,
    )
```

```python
import functools
import math

import jax
import jax.numpy as jnp
from jax import lax
from jax.experimental import pallas as pl
from jax.experimental.pallas import tpu as pltpu
from jax.sharding import PartitionSpec as P

MESH = pl.DeviceIdType.MESH

SWEEPS = 4


def lane_shifts(u):
    ny = u.shape[-1]
    lane = lax.broadcasted_iota(jnp.int32, u.shape, u.ndim - 1)
    fwd, back = pltpu.roll(u, 1, u.ndim - 1), pltpu.roll(u, ny - 1, u.ndim - 1)
    rolled = pltpu.roll(lane, 1, u.ndim - 1)
    moved = (rolled == lane - 1) | (rolled == lane + ny - 1)
    lower = jnp.where(moved, fwd, back)
    upper = jnp.where(moved, back, fwd)
    zero = jnp.zeros_like(u)
    return jnp.where(lane == 0, zero, lower), jnp.where(lane == ny - 1, zero, upper)


def row_shifts(u):
    zero = jnp.zeros_like(u[:1])
    return jnp.concatenate([zero, u[:-1]], axis=0), jnp.concatenate([u[1:], zero], axis=0)


def fused_kernel(half, width, factor, owner_hbm, diff_hbm, ctrl_hbm, mask_hbm, pert_hbm,
                 out_ref, owner_ref, diff_ref, ctrl_ref, mask_ref, ext, mext, held, pert,
                 send_sem, recv_sem, load_sem):
    tile = lax.axis_index("tile")
    count = lax.axis_size("tile")
    me = lax.axis_index("tm")
    groups = lax.axis_size("tm")
    depth, rows, lev, ny = ctrl_hbm.shape
    wide = rows + 2 * width
    right = lax.rem(tile + 1, count)
    left = lax.rem(tile + count - 1, count)
    zp = lax.rem(me + half, groups)
    base = me - lax.rem(me, half)
    peers = [base + lax.rem(lax.rem(me, half) + d, half) for d in range(1, half)]

    loads = [
        pltpu.make_async_copy(src, dst, load_sem.at[i])
        for i, (src, dst) in enumerate(
            [(ctrl_hbm, ctrl_ref), (mask_hbm, mask_ref), (diff_hbm, diff_ref),
             (owner_hbm, owner_ref), (pert_hbm, pert)]
        )
    ]
    for c in loads:
        c.start()
    for c in loads[:4]:
        c.wait()

    barrier = pltpu.get_barrier_semaphore()
    for dev in ((left, me), (right, me), (tile, zp)) + tuple((tile, p) for p in peers):
        pl.semaphore_signal(barrier, inc=1, device_id=dev, device_id_type=MESH)
    pl.semaphore_wait(barrier, 2 + half)

    head, tail = pl.ds(0, width), pl.ds(rows - width, width)
    plan = [
        (ctrl_ref.at[:, tail], ext.at[:, pl.ds(0, width)], right),
        (mask_ref.at[tail], mext.at[pl.ds(0, width)], right),
        (ctrl_ref.at[:, head], ext.at[:, pl.ds(width + rows, width)], left),
        (mask_ref.at[head], mext.at[pl.ds(width + rows, width)], left),
    ]
    halo = []
    for i, (src, dst, dev) in enumerate(plan):
        c = pltpu.make_async_remote_copy(
            src_ref=src, dst_ref=dst, send_sem=send_sem.at[i], recv_sem=recv_sem.at[i],
            device_id=(dev, me), device_id_type=MESH,
        )
        c.start()
        halo.append(c)
    ext[:, pl.ds(width, rows)] = ctrl_ref[...]
    mext[pl.ds(width, rows)] = mask_ref[...]
    for c in halo:
        c.wait_recv()

    grow = tile * rows - width + lax.broadcasted_iota(jnp.int32, (wide, lev, ny), 0)
    inside = (grow >= 0) & (grow < count * rows)
    levels = lax.broadcasted_iota(jnp.int32, (wide, lev, ny), 1)
    sea = jnp.zeros((wide, lev, ny), jnp.float32)
    land = jnp.zeros((wide, lev, ny), jnp.float32)
    for l in range(lev):
        sea = jnp.where(levels == l, diff_ref[0, l], sea)
        land = jnp.where(levels == l, diff_ref[1, l], land)
    landed = jnp.broadcast_to(mext[...][:, None, :], (wide, lev, ny)) == 1
    coef = jnp.where(inside, jnp.where(landed, land, sea), 0.0)
    cxm, cxp = row_shifts(coef)
    cym, cyp = lane_shifts(coef)
    axm, axp = 0.5 * (coef + cxm), 0.5 * (coef + cxp)
    aym, ayp = 0.5 * (coef + cym), 0.5 * (coef + cyp)

    def slot(g, k):
        return held.at[pl.ds(g * depth + k, 1)]

    def copy(g, k, dev, sem):
        return pltpu.make_async_remote_copy(
            src_ref=slot(g, k), dst_ref=slot(g, k), send_sem=send_sem.at[sem],
            recv_sem=recv_sem.at[4 + g * depth + k], device_id=(tile, dev), device_id_type=MESH,
        )

    def add(g, k):
        member = owner_ref[g * depth + k]
        out_ref[...] += pert[member].astype(jnp.float32) * held[g * depth + k].astype(jnp.float32)[None]

    sends = []
    for k in range(depth):
        u = jnp.where(inside, ext[k], 0.0)
        for sweep_index in range(SWEEPS):
            uxm, uxp = row_shifts(u)
            uym, uyp = lane_shifts(u)
            flux = axm * (uxm - u)
            flux = flux + axp * (uxp - u)
            flux = flux + aym * (uym - u)
            flux = flux + ayp * (uyp - u)
            u = jnp.where(inside, u + flux, 0.0)
        held[me * depth + k] = u[width:width + rows].astype(held.dtype)
        for i, p in enumerate([zp] + peers):
            c = copy(me, k, p, 4 + k * 2 * half + i)
            c.start()
            sends.append(c)

    for c in halo:
        c.wait_send()
    out_ref[...] = jnp.zeros(out_ref.shape, out_ref.dtype)
    loads[4].wait()
    for k in range(depth):
        add(me, k)
    for k in range(depth):
        copy(zp, k, zp, 4).wait_recv()
        for i, p in enumerate(peers):
            c = copy(zp, k, p, 4 + k * 2 * half + half + i)
            c.start()
            sends.append(c)
        add(zp, k)
    for p in peers:
        for g in (p, lax.rem(p + half, groups)):
            for k in range(depth):
                copy(g, k, p, 4).wait_recv()
                add(g, k)
    for c in sends:
        c.wait_send()
    out_ref[...] = out_ref[...] * factor


def on_device(controls, perturbations, owner, land_mask, diffusivity):
    groups = lax.axis_size("tm")
    half = 4 if groups % 4 == 0 else groups // 2
    depth, rows, lev, ny = controls.shape
    width = SWEEPS
    pert = perturbations[0]
    factor = 1.0 / math.sqrt(owner.shape[0] - 1)
    vmem = pl.BlockSpec(memory_space=pltpu.VMEM)
    hbm = pl.BlockSpec(memory_space=pl.ANY)
    out = pl.pallas_call(
        functools.partial(fused_kernel, half, width, factor),
        out_shape=jax.ShapeDtypeStruct(pert.shape[1:], jnp.float32),
        in_specs=[hbm] * 5,
        out_specs=vmem,
        scratch_shapes=[
            pltpu.SMEM(owner.shape, owner.dtype),
            pltpu.SMEM(diffusivity.shape, diffusivity.dtype),
            pltpu.VMEM(controls.shape, controls.dtype),
            pltpu.VMEM(land_mask.shape, land_mask.dtype),
            pltpu.VMEM((depth, rows + 2 * width, lev, ny), controls.dtype),
            pltpu.VMEM((rows + 2 * width, ny), land_mask.dtype),
            pltpu.VMEM((groups * depth, rows, lev, ny), jnp.bfloat16),
            pltpu.VMEM(pert.shape, pert.dtype),
            pltpu.SemaphoreType.DMA((4 + 2 * half * depth,)),
            pltpu.SemaphoreType.DMA((4 + groups * depth,)),
            pltpu.SemaphoreType.DMA((5,)),
        ],
        compiler_params=pltpu.CompilerParams(
            collective_id=0, has_side_effects=True, vmem_limit_bytes=64 * 1024 * 1024
        ),
    )(owner, diffusivity, controls, land_mask, pert)
    return out[None]


def solution(mesh):
    return jax.shard_map(
        on_device,
        mesh=mesh,
        in_specs=(
            P("tm", "tile", None, None),
            P("tm", None, None, "tile", None, None),
            P(),
            P("tile", None),
            P(),
        ),
        out_specs=P("tm", None, "tile", None, None),
        check_vma=False,
    )
```

```python
import functools
import math

import jax
import jax.numpy as jnp
from jax import lax
from jax.experimental import pallas as pl
from jax.experimental.pallas import tpu as pltpu
from jax.sharding import PartitionSpec as P

MESH = pl.DeviceIdType.MESH

SWEEPS = 4


def lane_shifts(u):
    ny = u.shape[-1]
    lane = lax.broadcasted_iota(jnp.int32, u.shape, u.ndim - 1)
    fwd, back = pltpu.roll(u, 1, u.ndim - 1), pltpu.roll(u, ny - 1, u.ndim - 1)
    rolled = pltpu.roll(lane, 1, u.ndim - 1)
    moved = (rolled == lane - 1) | (rolled == lane + ny - 1)
    lower = jnp.where(moved, fwd, back)
    upper = jnp.where(moved, back, fwd)
    zero = jnp.zeros_like(u)
    return jnp.where(lane == 0, zero, lower), jnp.where(lane == ny - 1, zero, upper)


def fused_kernel(half, width, factor, owner_hbm, diff_hbm, ctrl_hbm, mask_hbm, pert_hbm,
                 out_ref, owner_ref, diff_ref, ctrl_ref, mask_ref, ext, mext, held, pert,
                 send_sem, recv_sem, load_sem):
    tile = lax.axis_index("tile")
    count = lax.axis_size("tile")
    me = lax.axis_index("tm")
    groups = lax.axis_size("tm")
    depth, rows, lev, ny = ctrl_hbm.shape
    wide = rows + 2 * width
    right = lax.rem(tile + 1, count)
    left = lax.rem(tile + count - 1, count)
    zp = lax.rem(me + half, groups)
    base = me - lax.rem(me, half)
    peers = [base + lax.rem(lax.rem(me, half) + d, half) for d in range(1, half)]

    loads = [
        pltpu.make_async_copy(src, dst, load_sem.at[i])
        for i, (src, dst) in enumerate(
            [(ctrl_hbm, ctrl_ref), (mask_hbm, mask_ref), (diff_hbm, diff_ref),
             (owner_hbm, owner_ref), (pert_hbm, pert)]
        )
    ]
    for c in loads:
        c.start()
    for c in loads[:4]:
        c.wait()

    barrier = pltpu.get_barrier_semaphore()
    for dev in ((left, me), (right, me), (tile, zp)) + tuple((tile, p) for p in peers):
        pl.semaphore_signal(barrier, inc=1, device_id=dev, device_id_type=MESH)
    pl.semaphore_wait(barrier, 2 + half)

    head, tail = pl.ds(0, width), pl.ds(rows - width, width)
    plan = [
        (ctrl_ref.at[:, tail], ext.at[:, pl.ds(0, width)], right),
        (mask_ref.at[tail], mext.at[pl.ds(0, width)], right),
        (ctrl_ref.at[:, head], ext.at[:, pl.ds(width + rows, width)], left),
        (mask_ref.at[head], mext.at[pl.ds(width + rows, width)], left),
    ]
    halo = []
    for i, (src, dst, dev) in enumerate(plan):
        c = pltpu.make_async_remote_copy(
            src_ref=src, dst_ref=dst, send_sem=send_sem.at[i], recv_sem=recv_sem.at[i],
            device_id=(dev, me), device_id_type=MESH,
        )
        c.start()
        halo.append(c)
    ext[:, pl.ds(width, rows)] = ctrl_ref[...]
    mext[pl.ds(width, rows)] = mask_ref[...]
    for c in halo:
        c.wait_recv()

    grow = tile * rows - width + lax.broadcasted_iota(jnp.int32, (wide, lev, ny), 0)
    inside = (grow >= 0) & (grow < count * rows)
    levels = lax.broadcasted_iota(jnp.int32, (wide, lev, ny), 1)
    sea = jnp.zeros((wide, lev, ny), jnp.float32)
    land = jnp.zeros((wide, lev, ny), jnp.float32)
    for l in range(lev):
        sea = jnp.where(levels == l, diff_ref[0, l], sea)
        land = jnp.where(levels == l, diff_ref[1, l], land)
    landed = jnp.broadcast_to(mext[...][:, None, :], (wide, lev, ny)) == 1
    coef = jnp.where(inside, jnp.where(landed, land, sea), 0.0)
    mid = coef[1:-1]
    cym, cyp = lane_shifts(mid)
    axm, axp = 0.5 * (mid + coef[:-2]), 0.5 * (mid + coef[2:])
    aym, ayp = 0.5 * (mid + cym), 0.5 * (mid + cyp)
    kept = inside[1:-1]

    def slot(g, k):
        return held.at[pl.ds(g * depth + k, 1)]

    def copy(g, k, dev, sem):
        return pltpu.make_async_remote_copy(
            src_ref=slot(g, k), dst_ref=slot(g, k), send_sem=send_sem.at[sem],
            recv_sem=recv_sem.at[4 + g * depth + k], device_id=(tile, dev), device_id_type=MESH,
        )

    def add(g, k):
        member = owner_ref[g * depth + k]
        out_ref[...] += pert[member].astype(jnp.float32) * held[g * depth + k].astype(jnp.float32)[None]

    sends = []
    for k in range(depth):
        u = jnp.where(inside, ext[k], 0.0)
        for sweep_index in range(SWEEPS):
            lo, hi = sweep_index, wide - 2 - sweep_index
            centre = u[1:-1]
            uym, uyp = lane_shifts(centre)
            flux = axm[lo:hi] * (u[:-2] - centre)
            flux = flux + axp[lo:hi] * (u[2:] - centre)
            flux = flux + aym[lo:hi] * (uym - centre)
            flux = flux + ayp[lo:hi] * (uyp - centre)
            u = jnp.where(kept[lo:hi], centre + flux, 0.0)
        held[me * depth + k] = u.astype(held.dtype)
        for i, p in enumerate([zp] + peers):
            c = copy(me, k, p, 4 + k * 2 * half + i)
            c.start()
            sends.append(c)

    for c in halo:
        c.wait_send()
    out_ref[...] = jnp.zeros(out_ref.shape, out_ref.dtype)
    loads[4].wait()
    for k in range(depth):
        add(me, k)
    for k in range(depth):
        copy(zp, k, zp, 4).wait_recv()
        for i, p in enumerate(peers):
            c = copy(zp, k, p, 4 + k * 2 * half + half + i)
            c.start()
            sends.append(c)
        add(zp, k)
    for p in peers:
        for g in (p, lax.rem(p + half, groups)):
            for k in range(depth):
                copy(g, k, p, 4).wait_recv()
                add(g, k)
    for c in sends:
        c.wait_send()
    out_ref[...] = out_ref[...] * factor


def on_device(controls, perturbations, owner, land_mask, diffusivity):
    groups = lax.axis_size("tm")
    half = 4 if groups % 4 == 0 else groups // 2
    depth, rows, lev, ny = controls.shape
    width = SWEEPS
    pert = perturbations[0]
    factor = 1.0 / math.sqrt(owner.shape[0] - 1)
    vmem = pl.BlockSpec(memory_space=pltpu.VMEM)
    hbm = pl.BlockSpec(memory_space=pl.ANY)
    out = pl.pallas_call(
        functools.partial(fused_kernel, half, width, factor),
        out_shape=jax.ShapeDtypeStruct(pert.shape[1:], jnp.float32),
        in_specs=[hbm] * 5,
        out_specs=vmem,
        scratch_shapes=[
            pltpu.SMEM(owner.shape, owner.dtype),
            pltpu.SMEM(diffusivity.shape, diffusivity.dtype),
            pltpu.VMEM(controls.shape, controls.dtype),
            pltpu.VMEM(land_mask.shape, land_mask.dtype),
            pltpu.VMEM((depth, rows + 2 * width, lev, ny), controls.dtype),
            pltpu.VMEM((rows + 2 * width, ny), land_mask.dtype),
            pltpu.VMEM((groups * depth, rows, lev, ny), jnp.bfloat16),
            pltpu.VMEM(pert.shape, pert.dtype),
            pltpu.SemaphoreType.DMA((4 + 2 * half * depth,)),
            pltpu.SemaphoreType.DMA((4 + groups * depth,)),
            pltpu.SemaphoreType.DMA((5,)),
        ],
        compiler_params=pltpu.CompilerParams(
            collective_id=0, has_side_effects=True, vmem_limit_bytes=64 * 1024 * 1024
        ),
    )(owner, diffusivity, controls, land_mask, pert)
    return out[None]


def solution(mesh):
    return jax.shard_map(
        on_device,
        mesh=mesh,
        in_specs=(
            P("tm", "tile", None, None),
            P("tm", None, None, "tile", None, None),
            P(),
            P("tile", None),
            P(),
        ),
        out_specs=P("tm", None, "tile", None, None),
        check_vma=False,
    )
```

```python
import functools
import math

import jax
import jax.numpy as jnp
from jax import lax
from jax.experimental import pallas as pl
from jax.experimental.pallas import tpu as pltpu
from jax.sharding import PartitionSpec as P

MESH = pl.DeviceIdType.MESH

SWEEPS = 4


def lane_shifts(u):
    ny = u.shape[-1]
    lane = lax.broadcasted_iota(jnp.int32, u.shape, u.ndim - 1)
    fwd, back = pltpu.roll(u, 1, u.ndim - 1), pltpu.roll(u, ny - 1, u.ndim - 1)
    rolled = pltpu.roll(lane, 1, u.ndim - 1)
    moved = (rolled == lane - 1) | (rolled == lane + ny - 1)
    lower = jnp.where(moved, fwd, back)
    upper = jnp.where(moved, back, fwd)
    zero = jnp.zeros_like(u)
    return jnp.where(lane == 0, zero, lower), jnp.where(lane == ny - 1, zero, upper)


def fused_kernel(half, width, factor, owner_hbm, diff_hbm, ctrl_hbm, mask_hbm, pert_hbm,
                 out_ref, owner_ref, diff_ref, ctrl_ref, mask_ref, ext, mext, held, pert,
                 send_sem, recv_sem, load_sem):
    tile = lax.axis_index("tile")
    count = lax.axis_size("tile")
    me = lax.axis_index("tm")
    groups = lax.axis_size("tm")
    depth, rows, lev, ny = ctrl_hbm.shape
    wide = rows + 2 * width
    nhalo = 2 + 2 * depth
    right = lax.rem(tile + 1, count)
    left = lax.rem(tile + count - 1, count)
    zp = lax.rem(me + half, groups)
    base = me - lax.rem(me, half)
    peers = [base + lax.rem(lax.rem(me, half) + d, half) for d in range(1, half)]

    loads = [
        pltpu.make_async_copy(src, dst, load_sem.at[i])
        for i, (src, dst) in enumerate(
            [(ctrl_hbm, ctrl_ref), (mask_hbm, mask_ref), (diff_hbm, diff_ref),
             (owner_hbm, owner_ref), (pert_hbm, pert)]
        )
    ]
    for c in loads:
        c.start()
    for c in loads[:4]:
        c.wait()

    barrier = pltpu.get_barrier_semaphore()
    for dev in ((left, me), (right, me), (tile, zp)) + tuple((tile, p) for p in peers):
        pl.semaphore_signal(barrier, inc=1, device_id=dev, device_id_type=MESH)
    pl.semaphore_wait(barrier, 2 + half)

    head, tail = pl.ds(0, width), pl.ds(rows - width, width)
    before, after = pl.ds(0, width), pl.ds(width + rows, width)
    plan = [
        (mask_ref.at[tail], mext.at[before], right),
        (mask_ref.at[head], mext.at[after], left),
    ]
    for k in range(depth):
        plan.append((ctrl_ref.at[k, tail], ext.at[k, before], right))
        plan.append((ctrl_ref.at[k, head], ext.at[k, after], left))
    halo = []
    for i, (src, dst, dev) in enumerate(plan):
        c = pltpu.make_async_remote_copy(
            src_ref=src, dst_ref=dst, send_sem=send_sem.at[i], recv_sem=recv_sem.at[i],
            device_id=(dev, me), device_id_type=MESH,
        )
        c.start()
        halo.append(c)
    ext[:, pl.ds(width, rows)] = ctrl_ref[...]
    mext[pl.ds(width, rows)] = mask_ref[...]
    for c in halo[:2]:
        c.wait_recv()

    grow = tile * rows - width + lax.broadcasted_iota(jnp.int32, (wide, lev, ny), 0)
    inside = (grow >= 0) & (grow < count * rows)
    levels = lax.broadcasted_iota(jnp.int32, (wide, lev, ny), 1)
    sea = jnp.zeros((wide, lev, ny), jnp.float32)
    land = jnp.zeros((wide, lev, ny), jnp.float32)
    for l in range(lev):
        sea = jnp.where(levels == l, diff_ref[0, l], sea)
        land = jnp.where(levels == l, diff_ref[1, l], land)
    landed = jnp.broadcast_to(mext[...][:, None, :], (wide, lev, ny)) == 1
    coef = jnp.where(inside, jnp.where(landed, land, sea), 0.0)
    mid = coef[1:-1]
    cym, cyp = lane_shifts(mid)
    axm, axp = 0.5 * (mid + coef[:-2]), 0.5 * (mid + coef[2:])
    aym, ayp = 0.5 * (mid + cym), 0.5 * (mid + cyp)
    kept = inside[1:-1]

    def slot(g, k):
        return held.at[pl.ds(g * depth + k, 1)]

    def copy(g, k, dev, sem):
        return pltpu.make_async_remote_copy(
            src_ref=slot(g, k), dst_ref=slot(g, k), send_sem=send_sem.at[sem],
            recv_sem=recv_sem.at[nhalo + g * depth + k], device_id=(tile, dev), device_id_type=MESH,
        )

    def add(g, k):
        member = owner_ref[g * depth + k]
        out_ref[...] += pert[member].astype(jnp.float32) * held[g * depth + k].astype(jnp.float32)[None]

    sends = []
    for k in range(depth):
        for c in halo[2 + 2 * k:4 + 2 * k]:
            c.wait_recv()
        u = jnp.where(inside, ext[k], 0.0)
        for sweep_index in range(SWEEPS):
            lo, hi = sweep_index, wide - 2 - sweep_index
            centre = u[1:-1]
            uym, uyp = lane_shifts(centre)
            flux = axm[lo:hi] * (u[:-2] - centre)
            flux = flux + axp[lo:hi] * (u[2:] - centre)
            flux = flux + aym[lo:hi] * (uym - centre)
            flux = flux + ayp[lo:hi] * (uyp - centre)
            u = jnp.where(kept[lo:hi], centre + flux, 0.0)
        held[me * depth + k] = u.astype(held.dtype)
        for i, p in enumerate([zp] + peers):
            c = copy(me, k, p, nhalo + k * 2 * half + i)
            c.start()
            sends.append(c)

    for c in halo:
        c.wait_send()
    out_ref[...] = jnp.zeros(out_ref.shape, out_ref.dtype)
    loads[4].wait()
    for k in range(depth):
        add(me, k)
    for k in range(depth):
        copy(zp, k, zp, nhalo).wait_recv()
        for i, p in enumerate(peers):
            c = copy(zp, k, p, nhalo + k * 2 * half + half + i)
            c.start()
            sends.append(c)
        add(zp, k)
    for p in peers:
        for g in (p, lax.rem(p + half, groups)):
            for k in range(depth):
                copy(g, k, p, nhalo).wait_recv()
                add(g, k)
    for c in sends:
        c.wait_send()
    out_ref[...] = out_ref[...] * factor


def on_device(controls, perturbations, owner, land_mask, diffusivity):
    groups = lax.axis_size("tm")
    half = 4 if groups % 4 == 0 else groups // 2
    depth, rows, lev, ny = controls.shape
    width = SWEEPS
    pert = perturbations[0]
    factor = 1.0 / math.sqrt(owner.shape[0] - 1)
    vmem = pl.BlockSpec(memory_space=pltpu.VMEM)
    hbm = pl.BlockSpec(memory_space=pl.ANY)
    out = pl.pallas_call(
        functools.partial(fused_kernel, half, width, factor),
        out_shape=jax.ShapeDtypeStruct(pert.shape[1:], jnp.float32),
        in_specs=[hbm] * 5,
        out_specs=vmem,
        scratch_shapes=[
            pltpu.SMEM(owner.shape, owner.dtype),
            pltpu.SMEM(diffusivity.shape, diffusivity.dtype),
            pltpu.VMEM(controls.shape, controls.dtype),
            pltpu.VMEM(land_mask.shape, land_mask.dtype),
            pltpu.VMEM((depth, rows + 2 * width, lev, ny), controls.dtype),
            pltpu.VMEM((rows + 2 * width, ny), land_mask.dtype),
            pltpu.VMEM((groups * depth, rows, lev, ny), jnp.bfloat16),
            pltpu.VMEM(pert.shape, pert.dtype),
            pltpu.SemaphoreType.DMA((2 + 2 * depth + 2 * half * depth,)),
            pltpu.SemaphoreType.DMA((2 + 2 * depth + groups * depth,)),
            pltpu.SemaphoreType.DMA((5,)),
        ],
        compiler_params=pltpu.CompilerParams(
            collective_id=0, has_side_effects=True, vmem_limit_bytes=64 * 1024 * 1024
        ),
    )(owner, diffusivity, controls, land_mask, pert)
    return out[None]


def solution(mesh):
    return jax.shard_map(
        on_device,
        mesh=mesh,
        in_specs=(
            P("tm", "tile", None, None),
            P("tm", None, None, "tile", None, None),
            P(),
            P("tile", None),
            P(),
        ),
        out_specs=P("tm", None, "tile", None, None),
        check_vma=False,
    )
```

```python
import functools
import math

import jax
import jax.numpy as jnp
from jax import lax
from jax.experimental import pallas as pl
from jax.experimental.pallas import tpu as pltpu
from jax.sharding import PartitionSpec as P

MESH = pl.DeviceIdType.MESH

SWEEPS = 4


def lane_shifts(u):
    ny = u.shape[-1]
    lane = lax.broadcasted_iota(jnp.int32, u.shape, u.ndim - 1)
    fwd, back = pltpu.roll(u, 1, u.ndim - 1), pltpu.roll(u, ny - 1, u.ndim - 1)
    rolled = pltpu.roll(lane, 1, u.ndim - 1)
    moved = (rolled == lane - 1) | (rolled == lane + ny - 1)
    lower = jnp.where(moved, fwd, back)
    upper = jnp.where(moved, back, fwd)
    zero = jnp.zeros_like(u)
    return jnp.where(lane == 0, zero, lower), jnp.where(lane == ny - 1, zero, upper)


def fused_kernel(half, width, factor, owner_hbm, diff_hbm, ctrl_hbm, mask_hbm, pert_hbm,
                 out_ref, owner_ref, diff_ref, ctrl_ref, mask_ref, ext, mext, held, pert,
                 send_sem, recv_sem, load_sem):
    tile = lax.axis_index("tile")
    count = lax.axis_size("tile")
    me = lax.axis_index("tm")
    groups = lax.axis_size("tm")
    depth, rows, lev, ny = ctrl_hbm.shape
    wide = rows + 2 * width
    nhalo = 2 + 2 * depth
    right = lax.rem(tile + 1, count)
    left = lax.rem(tile + count - 1, count)
    zp = lax.rem(me + half, groups)
    base = me - lax.rem(me, half)
    peers = [base + lax.rem(lax.rem(me, half) + d, half) for d in range(1, half)]

    loads = [
        pltpu.make_async_copy(src, dst, load_sem.at[i])
        for i, (src, dst) in enumerate(
            [(ctrl_hbm, ctrl_ref), (mask_hbm, mask_ref), (diff_hbm, diff_ref),
             (owner_hbm, owner_ref), (pert_hbm, pert)]
        )
    ]
    for c in loads:
        c.start()
    for c in loads[:4]:
        c.wait()

    barrier = pltpu.get_barrier_semaphore()
    for dev in ((left, me), (right, me), (tile, zp)) + tuple((tile, p) for p in peers):
        pl.semaphore_signal(barrier, inc=1, device_id=dev, device_id_type=MESH)
    pl.semaphore_wait(barrier, 2 + half)

    head, tail = pl.ds(0, width), pl.ds(rows - width, width)
    before, after = pl.ds(0, width), pl.ds(width + rows, width)
    plan = [
        (mask_ref.at[tail], mext.at[before], right),
        (mask_ref.at[head], mext.at[after], left),
    ]
    for k in range(depth):
        plan.append((ctrl_ref.at[k, tail], ext.at[k, before], right))
        plan.append((ctrl_ref.at[k, head], ext.at[k, after], left))
    halo = []
    for i, (src, dst, dev) in enumerate(plan):
        c = pltpu.make_async_remote_copy(
            src_ref=src, dst_ref=dst, send_sem=send_sem.at[i], recv_sem=recv_sem.at[i],
            device_id=(dev, me), device_id_type=MESH,
        )
        c.start()
        halo.append(c)
    ext[:, pl.ds(width, rows)] = ctrl_ref[...]
    mext[pl.ds(width, rows)] = mask_ref[...]
    hr = rows // 2
    win = hr + 2 * width
    levels = lax.broadcasted_iota(jnp.int32, (win, lev, ny), 1)
    sea = jnp.zeros((win, lev, ny), jnp.float32)
    land = jnp.zeros((win, lev, ny), jnp.float32)
    for l in range(lev):
        sea = jnp.where(levels == l, diff_ref[0, l], sea)
        land = jnp.where(levels == l, diff_ref[1, l], land)

    def prep(h):
        grow = tile * rows - width + h * hr + lax.broadcasted_iota(jnp.int32, (win, lev, ny), 0)
        inside = (grow >= 0) & (grow < count * rows)
        landed = jnp.broadcast_to(mext[pl.ds(h * hr, win)][:, None, :], (win, lev, ny)) == 1
        coef = jnp.where(inside, jnp.where(landed, land, sea), 0.0)
        mid = coef[1:-1]
        cym, cyp = lane_shifts(mid)
        return (inside, inside[1:-1], 0.5 * (mid + coef[:-2]), 0.5 * (mid + coef[2:]),
                0.5 * (mid + cym), 0.5 * (mid + cyp))

    def smooth(k, h, prepped):
        inside, kept, axm, axp, aym, ayp = prepped
        u = jnp.where(inside, ext[k, pl.ds(h * hr, win)], 0.0)
        for sweep_index in range(SWEEPS):
            lo, hi = sweep_index, win - 2 - sweep_index
            centre = u[1:-1]
            uym, uyp = lane_shifts(centre)
            flux = axm[lo:hi] * (u[:-2] - centre)
            flux = flux + axp[lo:hi] * (u[2:] - centre)
            flux = flux + aym[lo:hi] * (uym - centre)
            flux = flux + ayp[lo:hi] * (uyp - centre)
            u = jnp.where(kept[lo:hi], centre + flux, 0.0)
        held[me * depth + k, pl.ds(h * hr, hr)] = u.astype(held.dtype)

    per = 2 * half - 1

    def copy(g, k, h, dev, sem):
        piece = held.at[pl.ds(g * depth + k, 1), pl.ds(h * hr, hr)]
        return pltpu.make_async_remote_copy(
            src_ref=piece, dst_ref=piece, send_sem=send_sem.at[nhalo + (k * 2 + h) * per + sem],
            recv_sem=recv_sem.at[nhalo + (g * depth + k) * 2 + h],
            device_id=(tile, dev), device_id_type=MESH,
        )

    def add(g, k):
        member = owner_ref[g * depth + k]
        out_ref[...] += pert[member].astype(jnp.float32) * held[g * depth + k].astype(jnp.float32)[None]

    def run(order):
        sends = []
        for h in order:
            halo[h].wait_recv()
            prepped = prep(h)
            for k in range(depth):
                halo[2 + 2 * k + h].wait_recv()
                smooth(k, h, prepped)
                for i, p in enumerate([zp] + peers):
                    c = copy(me, k, h, p, i)
                    c.start()
                    sends.append(c)
        for c in halo:
            c.wait_send()
        out_ref[...] = jnp.zeros(out_ref.shape, out_ref.dtype)
        loads[4].wait()
        for k in range(depth):
            add(me, k)
        for h in order:
            for k in range(depth):
                copy(zp, k, h, zp, 0).wait_recv()
                for i, p in enumerate(peers):
                    c = copy(zp, k, h, p, half + i)
                    c.start()
                    sends.append(c)
        for k in range(depth):
            add(zp, k)
        for p in peers:
            for g in (p, lax.rem(p + half, groups)):
                for h in order:
                    for k in range(depth):
                        copy(g, k, h, p, 0).wait_recv()
                for k in range(depth):
                    add(g, k)
        for c in sends:
            c.wait_send()
        out_ref[...] = out_ref[...] * factor

    core = lax.rem(tile, 2)

    @pl.when(core == 0)
    def _():
        run((1, 0))

    @pl.when(core == 1)
    def _():
        run((0, 1))

def on_device(controls, perturbations, owner, land_mask, diffusivity):
    groups = lax.axis_size("tm")
    half = 4 if groups % 4 == 0 else groups // 2
    depth, rows, lev, ny = controls.shape
    width = SWEEPS
    pert = perturbations[0]
    factor = 1.0 / math.sqrt(owner.shape[0] - 1)
    vmem = pl.BlockSpec(memory_space=pltpu.VMEM)
    hbm = pl.BlockSpec(memory_space=pl.ANY)
    out = pl.pallas_call(
        functools.partial(fused_kernel, half, width, factor),
        out_shape=jax.ShapeDtypeStruct(pert.shape[1:], jnp.float32),
        in_specs=[hbm] * 5,
        out_specs=vmem,
        scratch_shapes=[
            pltpu.SMEM(owner.shape, owner.dtype),
            pltpu.SMEM(diffusivity.shape, diffusivity.dtype),
            pltpu.VMEM(controls.shape, controls.dtype),
            pltpu.VMEM(land_mask.shape, land_mask.dtype),
            pltpu.VMEM((depth, rows + 2 * width, lev, ny), controls.dtype),
            pltpu.VMEM((rows + 2 * width, ny), land_mask.dtype),
            pltpu.VMEM((groups * depth, rows, lev, ny), jnp.bfloat16),
            pltpu.VMEM(pert.shape, pert.dtype),
            pltpu.SemaphoreType.DMA((2 + 2 * depth + 2 * depth * (2 * half - 1),)),
            pltpu.SemaphoreType.DMA((2 + 2 * depth + 2 * groups * depth,)),
            pltpu.SemaphoreType.DMA((5,)),
        ],
        compiler_params=pltpu.CompilerParams(
            collective_id=0, has_side_effects=True, vmem_limit_bytes=64 * 1024 * 1024
        ),
    )(owner, diffusivity, controls, land_mask, pert)
    return out[None]


def solution(mesh):
    return jax.shard_map(
        on_device,
        mesh=mesh,
        in_specs=(
            P("tm", "tile", None, None),
            P("tm", None, None, "tile", None, None),
            P(),
            P("tile", None),
            P(),
        ),
        out_specs=P("tm", None, "tile", None, None),
        check_vma=False,
    )
```

```python
import functools
import math

import jax
import jax.numpy as jnp
from jax import lax
from jax.experimental import pallas as pl
from jax.experimental.pallas import tpu as pltpu
from jax.sharding import PartitionSpec as P

MESH = pl.DeviceIdType.MESH

SWEEPS = 4


def lane_shifts(u):
    ny = u.shape[-1]
    lane = lax.broadcasted_iota(jnp.int32, u.shape, u.ndim - 1)
    fwd, back = pltpu.roll(u, 1, u.ndim - 1), pltpu.roll(u, ny - 1, u.ndim - 1)
    rolled = pltpu.roll(lane, 1, u.ndim - 1)
    moved = (rolled == lane - 1) | (rolled == lane + ny - 1)
    lower = jnp.where(moved, fwd, back)
    upper = jnp.where(moved, back, fwd)
    zero = jnp.zeros_like(u)
    return jnp.where(lane == 0, zero, lower), jnp.where(lane == ny - 1, zero, upper)


def fused_kernel(half, width, factor, owner_hbm, diff_hbm, ctrl_hbm, mask_hbm, pert_hbm,
                 out_ref, owner_ref, diff_ref, ext, mext, held, pert,
                 send_sem, recv_sem, load_sem):
    tile = lax.axis_index("tile")
    count = lax.axis_size("tile")
    me = lax.axis_index("tm")
    groups = lax.axis_size("tm")
    depth, rows, lev, ny = ctrl_hbm.shape
    wide = rows + 2 * width
    nhalo = 2 + 2 * depth
    right = lax.rem(tile + 1, count)
    left = lax.rem(tile + count - 1, count)
    zp = lax.rem(me + half, groups)
    base = me - lax.rem(me, half)
    peers = [base + lax.rem(lax.rem(me, half) + d, half) for d in range(1, half)]

    barrier = pltpu.get_barrier_semaphore()
    for dev in ((left, me), (right, me), (tile, zp)) + tuple((tile, p) for p in peers):
        pl.semaphore_signal(barrier, inc=1, device_id=dev, device_id_type=MESH)

    loads = [
        pltpu.make_async_copy(src, dst, load_sem.at[i])
        for i, (src, dst) in enumerate(
            [(ctrl_hbm, ext.at[:, pl.ds(width, rows)]), (mask_hbm, mext.at[pl.ds(width, rows)]),
             (diff_hbm, diff_ref), (owner_hbm, owner_ref), (pert_hbm, pert)]
        )
    ]
    for c in loads:
        c.start()
    pl.semaphore_wait(barrier, 2 + half)

    head, tail = pl.ds(0, width), pl.ds(rows - width, width)
    before, after = pl.ds(0, width), pl.ds(width + rows, width)
    plan = [
        (mask_hbm.at[tail], mext.at[before], right),
        (mask_hbm.at[head], mext.at[after], left),
    ]
    for k in range(depth):
        plan.append((ctrl_hbm.at[k, tail], ext.at[k, before], right))
        plan.append((ctrl_hbm.at[k, head], ext.at[k, after], left))
    halo = []
    for i, (src, dst, dev) in enumerate(plan):
        c = pltpu.make_async_remote_copy(
            src_ref=src, dst_ref=dst, send_sem=send_sem.at[i], recv_sem=recv_sem.at[i],
            device_id=(dev, me), device_id_type=MESH,
        )
        c.start()
        halo.append(c)
    for c in loads[:4]:
        c.wait()
    for c in halo[:2]:
        c.wait_recv()

    grow = tile * rows - width + lax.broadcasted_iota(jnp.int32, (wide, lev, ny), 0)
    inside = (grow >= 0) & (grow < count * rows)
    levels = lax.broadcasted_iota(jnp.int32, (wide, lev, ny), 1)
    sea = jnp.zeros((wide, lev, ny), jnp.float32)
    land = jnp.zeros((wide, lev, ny), jnp.float32)
    for l in range(lev):
        sea = jnp.where(levels == l, diff_ref[0, l], sea)
        land = jnp.where(levels == l, diff_ref[1, l], land)
    landed = jnp.broadcast_to(mext[...][:, None, :], (wide, lev, ny)) == 1
    coef = jnp.where(inside, jnp.where(landed, land, sea), 0.0)
    mid = coef[1:-1]
    cym, cyp = lane_shifts(mid)
    axm, axp = 0.5 * (mid + coef[:-2]), 0.5 * (mid + coef[2:])
    aym, ayp = 0.5 * (mid + cym), 0.5 * (mid + cyp)
    kept = inside[1:-1]

    def slot(g, k):
        return held.at[pl.ds(g * depth + k, 1)]

    def copy(g, k, dev, sem):
        return pltpu.make_async_remote_copy(
            src_ref=slot(g, k), dst_ref=slot(g, k), send_sem=send_sem.at[sem],
            recv_sem=recv_sem.at[nhalo + g * depth + k], device_id=(tile, dev), device_id_type=MESH,
        )

    def add(g, k):
        member = owner_ref[g * depth + k]
        out_ref[...] += pert[member].astype(jnp.float32) * held[g * depth + k].astype(jnp.float32)[None]

    sends = []
    for k in range(depth):
        for c in halo[2 + 2 * k:4 + 2 * k]:
            c.wait_recv()
        u = jnp.where(inside, ext[k], 0.0)
        for sweep_index in range(SWEEPS):
            lo, hi = sweep_index, wide - 2 - sweep_index
            centre = u[1:-1]
            uym, uyp = lane_shifts(centre)
            flux = axm[lo:hi] * (u[:-2] - centre)
            flux = flux + axp[lo:hi] * (u[2:] - centre)
            flux = flux + aym[lo:hi] * (uym - centre)
            flux = flux + ayp[lo:hi] * (uyp - centre)
            u = jnp.where(kept[lo:hi], centre + flux, 0.0)
        held[me * depth + k] = u.astype(held.dtype)
        for i, p in enumerate([zp] + peers):
            c = copy(me, k, p, nhalo + k * 2 * half + i)
            c.start()
            sends.append(c)

    for c in halo:
        c.wait_send()
    out_ref[...] = jnp.zeros(out_ref.shape, out_ref.dtype)
    loads[4].wait()
    for k in range(depth):
        add(me, k)
    for k in range(depth):
        copy(zp, k, zp, nhalo).wait_recv()
        for i, p in enumerate(peers):
            c = copy(zp, k, p, nhalo + k * 2 * half + half + i)
            c.start()
            sends.append(c)
        add(zp, k)
    for p in peers:
        for g in (p, lax.rem(p + half, groups)):
            for k in range(depth):
                copy(g, k, p, nhalo).wait_recv()
                add(g, k)
    for c in sends:
        c.wait_send()
    out_ref[...] = out_ref[...] * factor


def on_device(controls, perturbations, owner, land_mask, diffusivity):
    groups = lax.axis_size("tm")
    half = 4 if groups % 4 == 0 else groups // 2
    depth, rows, lev, ny = controls.shape
    width = SWEEPS
    pert = perturbations[0]
    factor = 1.0 / math.sqrt(owner.shape[0] - 1)
    vmem = pl.BlockSpec(memory_space=pltpu.VMEM)
    hbm = pl.BlockSpec(memory_space=pl.ANY)
    out = pl.pallas_call(
        functools.partial(fused_kernel, half, width, factor),
        out_shape=jax.ShapeDtypeStruct(pert.shape[1:], jnp.float32),
        in_specs=[hbm] * 5,
        out_specs=vmem,
        scratch_shapes=[
            pltpu.SMEM(owner.shape, owner.dtype),
            pltpu.SMEM(diffusivity.shape, diffusivity.dtype),
            pltpu.VMEM((depth, rows + 2 * width, lev, ny), controls.dtype),
            pltpu.VMEM((rows + 2 * width, ny), land_mask.dtype),
            pltpu.VMEM((groups * depth, rows, lev, ny), jnp.bfloat16),
            pltpu.VMEM(pert.shape, pert.dtype),
            pltpu.SemaphoreType.DMA((2 + 2 * depth + 2 * half * depth,)),
            pltpu.SemaphoreType.DMA((2 + 2 * depth + groups * depth,)),
            pltpu.SemaphoreType.DMA((5,)),
        ],
        compiler_params=pltpu.CompilerParams(
            collective_id=0, has_side_effects=True, vmem_limit_bytes=64 * 1024 * 1024
        ),
    )(owner, diffusivity, controls, land_mask, pert)
    return out[None]


def solution(mesh):
    return jax.shard_map(
        on_device,
        mesh=mesh,
        in_specs=(
            P("tm", "tile", None, None),
            P("tm", None, None, "tile", None, None),
            P(),
            P("tile", None),
            P(),
        ),
        out_specs=P("tm", None, "tile", None, None),
        check_vma=False,
    )
```

```python
import functools
import math

import jax
import jax.numpy as jnp
from jax import lax
from jax.experimental import pallas as pl
from jax.experimental.pallas import tpu as pltpu
from jax.sharding import PartitionSpec as P

MESH = pl.DeviceIdType.MESH

SWEEPS = 4


def lane_shifts(u):
    ny = u.shape[-1]
    lane = lax.broadcasted_iota(jnp.int32, u.shape, u.ndim - 1)
    fwd, back = pltpu.roll(u, 1, u.ndim - 1), pltpu.roll(u, ny - 1, u.ndim - 1)
    rolled = pltpu.roll(lane, 1, u.ndim - 1)
    moved = (rolled == lane - 1) | (rolled == lane + ny - 1)
    lower = jnp.where(moved, fwd, back)
    upper = jnp.where(moved, back, fwd)
    zero = jnp.zeros_like(u)
    return jnp.where(lane == 0, zero, lower), jnp.where(lane == ny - 1, zero, upper)


def fused_kernel(half, width, factor, owner_hbm, diff_hbm, ctrl_hbm, mask_hbm, pert_hbm,
                 out_ref, owner_ref, diff_ref, ext, mext, held, pert,
                 send_sem, recv_sem, load_sem):
    tile = lax.axis_index("tile")
    count = lax.axis_size("tile")
    me = lax.axis_index("tm")
    groups = lax.axis_size("tm")
    depth, rows, lev, ny = ctrl_hbm.shape
    wide = rows + 2 * width
    nhalo = 2 + 2 * depth
    right = lax.rem(tile + 1, count)
    left = lax.rem(tile + count - 1, count)
    zp = lax.rem(me + half, groups)
    base = me - lax.rem(me, half)
    peers = [base + lax.rem(lax.rem(me, half) + d, half) for d in range(1, half)]

    barrier = pltpu.get_barrier_semaphore()
    for dev in ((left, me), (right, me), (tile, zp)) + tuple((tile, p) for p in peers):
        pl.semaphore_signal(barrier, inc=1, device_id=dev, device_id_type=MESH)

    loads = [
        pltpu.make_async_copy(src, dst, load_sem.at[i])
        for i, (src, dst) in enumerate(
            [(ctrl_hbm, ext.at[:, pl.ds(width, rows)]), (mask_hbm, mext.at[pl.ds(width, rows)]),
             (diff_hbm, diff_ref), (owner_hbm, owner_ref), (pert_hbm, pert)]
        )
    ]
    for c in loads:
        c.start()
    pl.semaphore_wait(barrier, 2 + half)

    head, tail = pl.ds(0, width), pl.ds(rows - width, width)
    before, after = pl.ds(0, width), pl.ds(width + rows, width)
    plan = [
        (mask_hbm.at[tail], mext.at[before], right),
        (mask_hbm.at[head], mext.at[after], left),
    ]
    for k in range(depth):
        plan.append((ctrl_hbm.at[k, tail], ext.at[k, before], right))
        plan.append((ctrl_hbm.at[k, head], ext.at[k, after], left))
    halo = []
    for i, (src, dst, dev) in enumerate(plan):
        c = pltpu.make_async_remote_copy(
            src_ref=src, dst_ref=dst, send_sem=send_sem.at[i], recv_sem=recv_sem.at[i],
            device_id=(dev, me), device_id_type=MESH,
        )
        c.start()
        halo.append(c)
    for c in loads[:4]:
        c.wait()
    for c in halo[:2]:
        c.wait_recv()

    grow = tile * rows - width + lax.broadcasted_iota(jnp.int32, (wide, lev, ny), 0)
    inside = (grow >= 0) & (grow < count * rows)
    levels = lax.broadcasted_iota(jnp.int32, (wide, lev, ny), 1)
    sea = jnp.zeros((wide, lev, ny), jnp.float32)
    land = jnp.zeros((wide, lev, ny), jnp.float32)
    for l in range(lev):
        sea = jnp.where(levels == l, diff_ref[0, l], sea)
        land = jnp.where(levels == l, diff_ref[1, l], land)
    landed = jnp.broadcast_to(mext[...][:, None, :], (wide, lev, ny)) == 1
    coef = jnp.where(inside, jnp.where(landed, land, sea), 0.0)
    mid = coef[1:-1]
    cym, cyp = lane_shifts(mid)
    axm, axp = 0.5 * (mid + coef[:-2]), 0.5 * (mid + coef[2:])
    aym, ayp = 0.5 * (mid + cym), 0.5 * (mid + cyp)
    kept = inside[1:-1]

    def slot(g, k):
        return held.at[pl.ds(g * depth + k, 1)]

    def copy(g, k, dev, sem):
        return pltpu.make_async_remote_copy(
            src_ref=slot(g, k), dst_ref=slot(g, k), send_sem=send_sem.at[sem],
            recv_sem=recv_sem.at[nhalo + g * depth + k], device_id=(tile, dev), device_id_type=MESH,
        )

    def add(g, k, scale=None):
        member = owner_ref[g * depth + k]
        total = out_ref[...] + pert[member].astype(jnp.float32) * held[g * depth + k].astype(jnp.float32)[None]
        out_ref[...] = total if scale is None else total * scale

    sends = []
    for k in range(depth):
        for c in halo[2 + 2 * k:4 + 2 * k]:
            c.wait_recv()
        u = jnp.where(inside, ext[k], 0.0)
        for sweep_index in range(SWEEPS):
            lo, hi = sweep_index, wide - 2 - sweep_index
            centre = u[1:-1]
            uym, uyp = lane_shifts(centre)
            flux = axm[lo:hi] * (u[:-2] - centre)
            flux = flux + axp[lo:hi] * (u[2:] - centre)
            flux = flux + aym[lo:hi] * (uym - centre)
            flux = flux + ayp[lo:hi] * (uyp - centre)
            u = jnp.where(kept[lo:hi], centre + flux, 0.0)
        held[me * depth + k] = u.astype(held.dtype)
        for i, p in enumerate([zp] + peers):
            c = copy(me, k, p, nhalo + k * 2 * half + i)
            c.start()
            sends.append(c)

    for c in halo:
        c.wait_send()
    out_ref[...] = jnp.zeros(out_ref.shape, out_ref.dtype)
    loads[4].wait()
    for k in range(depth):
        add(me, k)
    for k in range(depth):
        copy(zp, k, zp, nhalo).wait_recv()
        for i, p in enumerate(peers):
            c = copy(zp, k, p, nhalo + k * 2 * half + half + i)
            c.start()
            sends.append(c)
        add(zp, k)
    for p in peers:
        for k in range(depth):
            copy(p, k, p, nhalo).wait_recv()
            add(p, k)
    for j, p in enumerate(peers):
        far = lax.rem(p + half, groups)
        for k in range(depth):
            copy(far, k, p, nhalo).wait_recv()
            last = j == len(peers) - 1 and k == depth - 1
            add(far, k, factor if last else None)
    for c in sends:
        c.wait_send()


def on_device(controls, perturbations, owner, land_mask, diffusivity):
    groups = lax.axis_size("tm")
    half = 4 if groups % 4 == 0 else groups // 2
    depth, rows, lev, ny = controls.shape
    width = SWEEPS
    pert = perturbations[0]
    factor = 1.0 / math.sqrt(owner.shape[0] - 1)
    vmem = pl.BlockSpec(memory_space=pltpu.VMEM)
    hbm = pl.BlockSpec(memory_space=pl.ANY)
    out = pl.pallas_call(
        functools.partial(fused_kernel, half, width, factor),
        out_shape=jax.ShapeDtypeStruct(pert.shape[1:], jnp.float32),
        in_specs=[hbm] * 5,
        out_specs=vmem,
        scratch_shapes=[
            pltpu.SMEM(owner.shape, owner.dtype),
            pltpu.SMEM(diffusivity.shape, diffusivity.dtype),
            pltpu.VMEM((depth, rows + 2 * width, lev, ny), controls.dtype),
            pltpu.VMEM((rows + 2 * width, ny), land_mask.dtype),
            pltpu.VMEM((groups * depth, rows, lev, ny), jnp.bfloat16),
            pltpu.VMEM(pert.shape, pert.dtype),
            pltpu.SemaphoreType.DMA((2 + 2 * depth + 2 * half * depth,)),
            pltpu.SemaphoreType.DMA((2 + 2 * depth + groups * depth,)),
            pltpu.SemaphoreType.DMA((5,)),
        ],
        compiler_params=pltpu.CompilerParams(
            collective_id=0, has_side_effects=True, vmem_limit_bytes=64 * 1024 * 1024
        ),
    )(owner, diffusivity, controls, land_mask, pert)
    return out[None]


def solution(mesh):
    return jax.shard_map(
        on_device,
        mesh=mesh,
        in_specs=(
            P("tm", "tile", None, None),
            P("tm", None, None, "tile", None, None),
            P(),
            P("tile", None),
            P(),
        ),
        out_specs=P("tm", None, "tile", None, None),
        check_vma=False,
    )
```

```python
import functools
import math

import jax
import jax.numpy as jnp
from jax import lax
from jax.experimental import pallas as pl
from jax.experimental.pallas import tpu as pltpu
from jax.sharding import PartitionSpec as P

MESH = pl.DeviceIdType.MESH

SWEEPS = 4


def lane_shifts(u):
    ny = u.shape[-1]
    lane = lax.broadcasted_iota(jnp.int32, u.shape, u.ndim - 1)
    fwd, back = pltpu.roll(u, 1, u.ndim - 1), pltpu.roll(u, ny - 1, u.ndim - 1)
    rolled = pltpu.roll(lane, 1, u.ndim - 1)
    moved = (rolled == lane - 1) | (rolled == lane + ny - 1)
    lower = jnp.where(moved, fwd, back)
    upper = jnp.where(moved, back, fwd)
    zero = jnp.zeros_like(u)
    return jnp.where(lane == 0, zero, lower), jnp.where(lane == ny - 1, zero, upper)


def fused_kernel(half, width, factor, owner_hbm, diff_hbm, ctrl_hbm, mask_hbm, pert_hbm,
                 out_hbm, owner_ref, diff_ref, ext, mext, held, pert, out_ref,
                 send_sem, recv_sem, load_sem):
    tile = lax.axis_index("tile")
    count = lax.axis_size("tile")
    me = lax.axis_index("tm")
    groups = lax.axis_size("tm")
    depth, rows, lev, ny = ctrl_hbm.shape
    wide = rows + 2 * width
    nhalo = 2 + 2 * depth
    right = lax.rem(tile + 1, count)
    left = lax.rem(tile + count - 1, count)
    zp = lax.rem(me + half, groups)
    base = me - lax.rem(me, half)
    peers = [base + lax.rem(lax.rem(me, half) + d, half) for d in range(1, half)]

    barrier = pltpu.get_barrier_semaphore()
    for dev in ((left, me), (right, me), (tile, zp)) + tuple((tile, p) for p in peers):
        pl.semaphore_signal(barrier, inc=1, device_id=dev, device_id_type=MESH)

    loads = [
        pltpu.make_async_copy(src, dst, load_sem.at[i])
        for i, (src, dst) in enumerate(
            [(ctrl_hbm, ext.at[:, pl.ds(width, rows)]), (mask_hbm, mext.at[pl.ds(width, rows)]),
             (diff_hbm, diff_ref), (owner_hbm, owner_ref), (pert_hbm, pert)]
        )
    ]
    for c in loads:
        c.start()
    pl.semaphore_wait(barrier, 2 + half)

    head, tail = pl.ds(0, width), pl.ds(rows - width, width)
    before, after = pl.ds(0, width), pl.ds(width + rows, width)
    plan = [
        (mask_hbm.at[tail], mext.at[before], right),
        (mask_hbm.at[head], mext.at[after], left),
    ]
    for k in range(depth):
        plan.append((ctrl_hbm.at[k, tail], ext.at[k, before], right))
        plan.append((ctrl_hbm.at[k, head], ext.at[k, after], left))
    halo = []
    for i, (src, dst, dev) in enumerate(plan):
        c = pltpu.make_async_remote_copy(
            src_ref=src, dst_ref=dst, send_sem=send_sem.at[i], recv_sem=recv_sem.at[i],
            device_id=(dev, me), device_id_type=MESH,
        )
        c.start()
        halo.append(c)
    for c in loads[:4]:
        c.wait()
    for c in halo[:2]:
        c.wait_recv()

    grow = tile * rows - width + lax.broadcasted_iota(jnp.int32, (wide, lev, ny), 0)
    inside = (grow >= 0) & (grow < count * rows)
    levels = lax.broadcasted_iota(jnp.int32, (wide, lev, ny), 1)
    sea = jnp.zeros((wide, lev, ny), jnp.float32)
    land = jnp.zeros((wide, lev, ny), jnp.float32)
    for l in range(lev):
        sea = jnp.where(levels == l, diff_ref[0, l], sea)
        land = jnp.where(levels == l, diff_ref[1, l], land)
    landed = jnp.broadcast_to(mext[...][:, None, :], (wide, lev, ny)) == 1
    coef = jnp.where(inside, jnp.where(landed, land, sea), 0.0)
    mid = coef[1:-1]
    cym, cyp = lane_shifts(mid)
    axm, axp = 0.5 * (mid + coef[:-2]), 0.5 * (mid + coef[2:])
    aym, ayp = 0.5 * (mid + cym), 0.5 * (mid + cyp)
    kept = inside[1:-1]

    def slot(g, k):
        return held.at[pl.ds(g * depth + k, 1)]

    def copy(g, k, dev, sem):
        return pltpu.make_async_remote_copy(
            src_ref=slot(g, k), dst_ref=slot(g, k), send_sem=send_sem.at[sem],
            recv_sem=recv_sem.at[nhalo + g * depth + k], device_id=(tile, dev), device_id_type=MESH,
        )

    def add(g, k, scale=None):
        member = owner_ref[g * depth + k]
        total = out_ref[...] + pert[member].astype(jnp.float32) * held[g * depth + k].astype(jnp.float32)[None]
        out_ref[...] = total if scale is None else total * scale

    sends = []
    for k in range(depth):
        for c in halo[2 + 2 * k:4 + 2 * k]:
            c.wait_recv()
        u = jnp.where(inside, ext[k], 0.0)
        for sweep_index in range(SWEEPS):
            lo, hi = sweep_index, wide - 2 - sweep_index
            centre = u[1:-1]
            uym, uyp = lane_shifts(centre)
            flux = axm[lo:hi] * (u[:-2] - centre)
            flux = flux + axp[lo:hi] * (u[2:] - centre)
            flux = flux + aym[lo:hi] * (uym - centre)
            flux = flux + ayp[lo:hi] * (uyp - centre)
            u = jnp.where(kept[lo:hi], centre + flux, 0.0)
        held[me * depth + k] = u.astype(held.dtype)
        for i, p in enumerate([zp] + peers):
            c = copy(me, k, p, nhalo + k * 2 * half + i)
            c.start()
            sends.append(c)

    for c in halo:
        c.wait_send()
    out_ref[...] = jnp.zeros(out_ref.shape, out_ref.dtype)
    loads[4].wait()
    for k in range(depth):
        add(me, k)
    for k in range(depth):
        copy(zp, k, zp, nhalo).wait_recv()
        for i, p in enumerate(peers):
            c = copy(zp, k, p, nhalo + k * 2 * half + half + i)
            c.start()
            sends.append(c)
        add(zp, k)
    for p in peers:
        for k in range(depth):
            copy(p, k, p, nhalo).wait_recv()
            add(p, k)
    for j, p in enumerate(peers):
        far = lax.rem(p + half, groups)
        for k in range(depth):
            copy(far, k, p, nhalo).wait_recv()
            last = j == len(peers) - 1 and k == depth - 1
            add(far, k, factor if last else None)
    store = pltpu.make_async_copy(out_ref, out_hbm, load_sem.at[5])
    store.start()
    for c in sends:
        c.wait_send()
    store.wait()


def on_device(controls, perturbations, owner, land_mask, diffusivity):
    groups = lax.axis_size("tm")
    half = 4 if groups % 4 == 0 else groups // 2
    depth, rows, lev, ny = controls.shape
    width = SWEEPS
    pert = perturbations[0]
    factor = 1.0 / math.sqrt(owner.shape[0] - 1)
    vmem = pl.BlockSpec(memory_space=pltpu.VMEM)
    hbm = pl.BlockSpec(memory_space=pl.ANY)
    out = pl.pallas_call(
        functools.partial(fused_kernel, half, width, factor),
        out_shape=jax.ShapeDtypeStruct(pert.shape[1:], jnp.float32),
        in_specs=[hbm] * 5,
        out_specs=hbm,
        scratch_shapes=[
            pltpu.SMEM(owner.shape, owner.dtype),
            pltpu.SMEM(diffusivity.shape, diffusivity.dtype),
            pltpu.VMEM((depth, rows + 2 * width, lev, ny), controls.dtype),
            pltpu.VMEM((rows + 2 * width, ny), land_mask.dtype),
            pltpu.VMEM((groups * depth, rows, lev, ny), jnp.bfloat16),
            pltpu.VMEM(pert.shape, pert.dtype),
            pltpu.VMEM(pert.shape[1:], jnp.float32),
            pltpu.SemaphoreType.DMA((2 + 2 * depth + 2 * half * depth,)),
            pltpu.SemaphoreType.DMA((2 + 2 * depth + groups * depth,)),
            pltpu.SemaphoreType.DMA((6,)),
        ],
        compiler_params=pltpu.CompilerParams(
            collective_id=0, has_side_effects=True, vmem_limit_bytes=64 * 1024 * 1024
        ),
    )(owner, diffusivity, controls, land_mask, pert)
    return out[None]


def solution(mesh):
    return jax.shard_map(
        on_device,
        mesh=mesh,
        in_specs=(
            P("tm", "tile", None, None),
            P("tm", None, None, "tile", None, None),
            P(),
            P("tile", None),
            P(),
        ),
        out_specs=P("tm", None, "tile", None, None),
        check_vma=False,
    )
```

```python
import functools
import math

import jax
import jax.numpy as jnp
from jax import lax
from jax.experimental import pallas as pl
from jax.experimental.pallas import tpu as pltpu
from jax.sharding import PartitionSpec as P

MESH = pl.DeviceIdType.MESH

SWEEPS = 4


def lane_shifts(u):
    ny = u.shape[-1]
    lane = lax.broadcasted_iota(jnp.int32, u.shape, u.ndim - 1)
    fwd, back = pltpu.roll(u, 1, u.ndim - 1), pltpu.roll(u, ny - 1, u.ndim - 1)
    rolled = pltpu.roll(lane, 1, u.ndim - 1)
    moved = (rolled == lane - 1) | (rolled == lane + ny - 1)
    lower = jnp.where(moved, fwd, back)
    upper = jnp.where(moved, back, fwd)
    zero = jnp.zeros_like(u)
    return jnp.where(lane == 0, zero, lower), jnp.where(lane == ny - 1, zero, upper)


def fused_kernel(half, width, factor, owner_hbm, diff_hbm, ctrl_hbm, mask_hbm, pert_hbm,
                 out_ref, owner_ref, diff_ref, ext, mext, held, pert,
                 send_sem, recv_sem, load_sem):
    tile = lax.axis_index("tile")
    count = lax.axis_size("tile")
    me = lax.axis_index("tm")
    groups = lax.axis_size("tm")
    depth, rows, lev, ny = ctrl_hbm.shape
    wide = rows + 2 * width
    nhalo = 2 + 2 * depth
    right = lax.rem(tile + 1, count)
    left = lax.rem(tile + count - 1, count)
    zp = lax.rem(me + half, groups)
    base = me - lax.rem(me, half)
    peers = [base + lax.rem(lax.rem(me, half) + d, half) for d in range(1, half)]

    barrier = pltpu.get_barrier_semaphore()
    for dev in ((left, me), (right, me), (tile, zp)) + tuple((tile, p) for p in peers):
        pl.semaphore_signal(barrier, inc=1, device_id=dev, device_id_type=MESH)

    loads = [
        pltpu.make_async_copy(src, dst, load_sem.at[i])
        for i, (src, dst) in enumerate(
            [(ctrl_hbm, ext.at[:, pl.ds(width, rows)]), (mask_hbm, mext.at[pl.ds(width, rows)]),
             (diff_hbm, diff_ref), (owner_hbm, owner_ref), (pert_hbm, pert)]
        )
    ]
    for c in loads:
        c.start()
    pl.semaphore_wait(barrier, 2 + half)

    head, tail = pl.ds(0, width), pl.ds(rows - width, width)
    before, after = pl.ds(0, width), pl.ds(width + rows, width)
    plan = [
        (mask_hbm.at[tail], mext.at[before], right),
        (mask_hbm.at[head], mext.at[after], left),
    ]
    for k in range(depth):
        plan.append((ctrl_hbm.at[k, tail], ext.at[k, before], right))
        plan.append((ctrl_hbm.at[k, head], ext.at[k, after], left))
    halo = []
    for i, (src, dst, dev) in enumerate(plan):
        c = pltpu.make_async_remote_copy(
            src_ref=src, dst_ref=dst, send_sem=send_sem.at[i], recv_sem=recv_sem.at[i],
            device_id=(dev, me), device_id_type=MESH,
        )
        c.start()
        halo.append(c)
    for c in loads[:4]:
        c.wait()
    for c in halo[:2]:
        c.wait_recv()

    grow = tile * rows - width + lax.broadcasted_iota(jnp.int32, (wide, lev, ny), 0)
    inside = (grow >= 0) & (grow < count * rows)
    levels = lax.broadcasted_iota(jnp.int32, (wide, lev, ny), 1)
    sea = jnp.zeros((wide, lev, ny), jnp.float32)
    land = jnp.zeros((wide, lev, ny), jnp.float32)
    for l in range(lev):
        sea = jnp.where(levels == l, diff_ref[0, l], sea)
        land = jnp.where(levels == l, diff_ref[1, l], land)
    landed = jnp.broadcast_to(mext[...][:, None, :], (wide, lev, ny)) == 1
    coef = jnp.where(inside, jnp.where(landed, land, sea), 0.0)
    mid = coef[1:-1]
    cym, cyp = lane_shifts(mid)
    axm, axp = 0.5 * (mid + coef[:-2]), 0.5 * (mid + coef[2:])
    aym, ayp = 0.5 * (mid + cym), 0.5 * (mid + cyp)
    kept = inside[1:-1]

    def slot(g, k):
        return held.at[pl.ds(g * depth + k, 1)]

    def copy(g, k, dev, sem):
        return pltpu.make_async_remote_copy(
            src_ref=slot(g, k), dst_ref=slot(g, k), send_sem=send_sem.at[sem],
            recv_sem=recv_sem.at[nhalo + g * depth + k], device_id=(tile, dev), device_id_type=MESH,
        )

    def add(g, k, scale=None):
        member = owner_ref[g * depth + k]
        total = out_ref[...] + pert[member].astype(jnp.float32) * held[g * depth + k].astype(jnp.float32)[None]
        out_ref[...] = total if scale is None else total * scale

    sends = []
    for k in range(depth):
        for c in halo[2 + 2 * k:4 + 2 * k]:
            c.wait_recv()
        u = jnp.where(inside, ext[k], 0.0)
        for sweep_index in range(SWEEPS):
            lo, hi = sweep_index, wide - 2 - sweep_index
            centre = u[1:-1]
            uym, uyp = lane_shifts(centre)
            flux = axm[lo:hi] * (u[:-2] - centre)
            flux = flux + axp[lo:hi] * (u[2:] - centre)
            flux = flux + aym[lo:hi] * (uym - centre)
            flux = flux + ayp[lo:hi] * (uyp - centre)
            u = jnp.where(kept[lo:hi], centre + flux, 0.0)
        held[me * depth + k] = u.astype(held.dtype)
        c = copy(me, k, zp, nhalo + k * 2 * half)
        c.start()
        sends.append(c)
    for k in range(depth):
        for i, p in enumerate(peers):
            c = copy(me, k, p, nhalo + k * 2 * half + 1 + i)
            c.start()
            sends.append(c)

    for c in halo:
        c.wait_send()
    out_ref[...] = jnp.zeros(out_ref.shape, out_ref.dtype)
    loads[4].wait()
    for k in range(depth):
        add(me, k)
    for k in range(depth):
        copy(zp, k, zp, nhalo).wait_recv()
        for i, p in enumerate(peers):
            c = copy(zp, k, p, nhalo + k * 2 * half + half + i)
            c.start()
            sends.append(c)
        add(zp, k)
    for p in peers:
        for k in range(depth):
            copy(p, k, p, nhalo).wait_recv()
            add(p, k)
    for j, p in enumerate(peers):
        far = lax.rem(p + half, groups)
        for k in range(depth):
            copy(far, k, p, nhalo).wait_recv()
            last = j == len(peers) - 1 and k == depth - 1
            add(far, k, factor if last else None)
    for c in sends:
        c.wait_send()


def on_device(controls, perturbations, owner, land_mask, diffusivity):
    groups = lax.axis_size("tm")
    half = 4 if groups % 4 == 0 else groups // 2
    depth, rows, lev, ny = controls.shape
    width = SWEEPS
    pert = perturbations[0]
    factor = 1.0 / math.sqrt(owner.shape[0] - 1)
    vmem = pl.BlockSpec(memory_space=pltpu.VMEM)
    hbm = pl.BlockSpec(memory_space=pl.ANY)
    out = pl.pallas_call(
        functools.partial(fused_kernel, half, width, factor),
        out_shape=jax.ShapeDtypeStruct(pert.shape[1:], jnp.float32),
        in_specs=[hbm] * 5,
        out_specs=vmem,
        scratch_shapes=[
            pltpu.SMEM(owner.shape, owner.dtype),
            pltpu.SMEM(diffusivity.shape, diffusivity.dtype),
            pltpu.VMEM((depth, rows + 2 * width, lev, ny), controls.dtype),
            pltpu.VMEM((rows + 2 * width, ny), land_mask.dtype),
            pltpu.VMEM((groups * depth, rows, lev, ny), jnp.bfloat16),
            pltpu.VMEM(pert.shape, pert.dtype),
            pltpu.SemaphoreType.DMA((2 + 2 * depth + 2 * half * depth,)),
            pltpu.SemaphoreType.DMA((2 + 2 * depth + groups * depth,)),
            pltpu.SemaphoreType.DMA((5,)),
        ],
        compiler_params=pltpu.CompilerParams(
            collective_id=0, has_side_effects=True, vmem_limit_bytes=64 * 1024 * 1024
        ),
    )(owner, diffusivity, controls, land_mask, pert)
    return out[None]


def solution(mesh):
    return jax.shard_map(
        on_device,
        mesh=mesh,
        in_specs=(
            P("tm", "tile", None, None),
            P("tm", None, None, "tile", None, None),
            P(),
            P("tile", None),
            P(),
        ),
        out_specs=P("tm", None, "tile", None, None),
        check_vma=False,
    )
```

```python
import functools
import math

import jax
import jax.numpy as jnp
from jax import lax
from jax.experimental import pallas as pl
from jax.experimental.pallas import tpu as pltpu
from jax.sharding import PartitionSpec as P

MESH = pl.DeviceIdType.MESH

SWEEPS = 4


def lane_shifts(u):
    ny = u.shape[-1]
    lane = lax.broadcasted_iota(jnp.int32, u.shape, u.ndim - 1)
    fwd, back = pltpu.roll(u, 1, u.ndim - 1), pltpu.roll(u, ny - 1, u.ndim - 1)
    rolled = pltpu.roll(lane, 1, u.ndim - 1)
    moved = (rolled == lane - 1) | (rolled == lane + ny - 1)
    lower = jnp.where(moved, fwd, back)
    upper = jnp.where(moved, back, fwd)
    zero = jnp.zeros_like(u)
    return jnp.where(lane == 0, zero, lower), jnp.where(lane == ny - 1, zero, upper)


def fused_kernel(half, width, factor, owner_hbm, diff_hbm, ctrl_hbm, mask_hbm, pert_hbm,
                 out_ref, owner_ref, diff_ref, ext, mext, held, pert,
                 send_sem, recv_sem, load_sem):
    tile = lax.axis_index("tile")
    count = lax.axis_size("tile")
    me = lax.axis_index("tm")
    groups = lax.axis_size("tm")
    depth, rows, lev, ny = ctrl_hbm.shape
    wide = rows + 2 * width
    nhalo = 2 + 2 * depth
    right = lax.rem(tile + 1, count)
    left = lax.rem(tile + count - 1, count)
    zp = lax.rem(me + half, groups)
    base = me - lax.rem(me, half)
    peers = [base + lax.rem(lax.rem(me, half) + d, half) for d in range(1, half)]

    barrier = pltpu.get_barrier_semaphore()
    for dev in ((left, me), (right, me), (tile, zp)) + tuple((tile, p) for p in peers):
        pl.semaphore_signal(barrier, inc=1, device_id=dev, device_id_type=MESH)

    loads = [
        pltpu.make_async_copy(src, dst, load_sem.at[i])
        for i, (src, dst) in enumerate(
            [(ctrl_hbm, ext.at[:, pl.ds(width, rows)]), (mask_hbm, mext.at[pl.ds(width, rows)]),
             (diff_hbm, diff_ref), (owner_hbm, owner_ref), (pert_hbm, pert)]
        )
    ]
    for c in loads[:4]:
        c.start()
    pl.semaphore_wait(barrier, 2 + half)

    head, tail = pl.ds(0, width), pl.ds(rows - width, width)
    before, after = pl.ds(0, width), pl.ds(width + rows, width)
    plan = [
        (mask_hbm.at[tail], mext.at[before], right),
        (mask_hbm.at[head], mext.at[after], left),
    ]
    for k in range(depth):
        plan.append((ctrl_hbm.at[k, tail], ext.at[k, before], right))
        plan.append((ctrl_hbm.at[k, head], ext.at[k, after], left))
    halo = []
    for i, (src, dst, dev) in enumerate(plan):
        c = pltpu.make_async_remote_copy(
            src_ref=src, dst_ref=dst, send_sem=send_sem.at[i], recv_sem=recv_sem.at[i],
            device_id=(dev, me), device_id_type=MESH,
        )
        c.start()
        halo.append(c)
    loads[4].start()
    for c in loads[:4]:
        c.wait()
    for c in halo[:2]:
        c.wait_recv()

    grow = tile * rows - width + lax.broadcasted_iota(jnp.int32, (wide, lev, ny), 0)
    inside = (grow >= 0) & (grow < count * rows)
    levels = lax.broadcasted_iota(jnp.int32, (wide, lev, ny), 1)
    sea = jnp.zeros((wide, lev, ny), jnp.float32)
    land = jnp.zeros((wide, lev, ny), jnp.float32)
    for l in range(lev):
        sea = jnp.where(levels == l, diff_ref[0, l], sea)
        land = jnp.where(levels == l, diff_ref[1, l], land)
    landed = jnp.broadcast_to(mext[...][:, None, :], (wide, lev, ny)) == 1
    coef = jnp.where(inside, jnp.where(landed, land, sea), 0.0)
    mid = coef[1:-1]
    cym, cyp = lane_shifts(mid)
    axm, axp = 0.5 * (mid + coef[:-2]), 0.5 * (mid + coef[2:])
    aym, ayp = 0.5 * (mid + cym), 0.5 * (mid + cyp)
    kept = inside[1:-1]

    def slot(g, k):
        return held.at[pl.ds(g * depth + k, 1)]

    def copy(g, k, dev, sem):
        return pltpu.make_async_remote_copy(
            src_ref=slot(g, k), dst_ref=slot(g, k), send_sem=send_sem.at[sem],
            recv_sem=recv_sem.at[nhalo + g * depth + k], device_id=(tile, dev), device_id_type=MESH,
        )

    def add(g, k, scale=None):
        member = owner_ref[g * depth + k]
        total = out_ref[...] + pert[member].astype(jnp.float32) * held[g * depth + k].astype(jnp.float32)[None]
        out_ref[...] = total if scale is None else total * scale

    sends = []
    for k in range(depth):
        for c in halo[2 + 2 * k:4 + 2 * k]:
            c.wait_recv()
        u = jnp.where(inside, ext[k], 0.0)
        for sweep_index in range(SWEEPS):
            lo, hi = sweep_index, wide - 2 - sweep_index
            centre = u[1:-1]
            uym, uyp = lane_shifts(centre)
            flux = axm[lo:hi] * (u[:-2] - centre)
            flux = flux + axp[lo:hi] * (u[2:] - centre)
            flux = flux + aym[lo:hi] * (uym - centre)
            flux = flux + ayp[lo:hi] * (uyp - centre)
            u = jnp.where(kept[lo:hi], centre + flux, 0.0)
        held[me * depth + k] = u.astype(held.dtype)
        for i, p in enumerate([zp] + peers):
            c = copy(me, k, p, nhalo + k * 2 * half + i)
            c.start()
            sends.append(c)

    for c in halo:
        c.wait_send()
    out_ref[...] = jnp.zeros(out_ref.shape, out_ref.dtype)
    loads[4].wait()
    for k in range(depth):
        add(me, k)
    for k in range(depth):
        copy(zp, k, zp, nhalo).wait_recv()
        for i, p in enumerate(peers):
            c = copy(zp, k, p, nhalo + k * 2 * half + half + i)
            c.start()
            sends.append(c)
        add(zp, k)
    for p in peers:
        for k in range(depth):
            copy(p, k, p, nhalo).wait_recv()
            add(p, k)
    for j, p in enumerate(peers):
        far = lax.rem(p + half, groups)
        for k in range(depth):
            copy(far, k, p, nhalo).wait_recv()
            last = j == len(peers) - 1 and k == depth - 1
            add(far, k, factor if last else None)
    for c in sends:
        c.wait_send()


def on_device(controls, perturbations, owner, land_mask, diffusivity):
    groups = lax.axis_size("tm")
    half = 4 if groups % 4 == 0 else groups // 2
    depth, rows, lev, ny = controls.shape
    width = SWEEPS
    pert = perturbations[0]
    factor = 1.0 / math.sqrt(owner.shape[0] - 1)
    vmem = pl.BlockSpec(memory_space=pltpu.VMEM)
    hbm = pl.BlockSpec(memory_space=pl.ANY)
    out = pl.pallas_call(
        functools.partial(fused_kernel, half, width, factor),
        out_shape=jax.ShapeDtypeStruct(pert.shape[1:], jnp.float32),
        in_specs=[hbm] * 5,
        out_specs=vmem,
        scratch_shapes=[
            pltpu.SMEM(owner.shape, owner.dtype),
            pltpu.SMEM(diffusivity.shape, diffusivity.dtype),
            pltpu.VMEM((depth, rows + 2 * width, lev, ny), controls.dtype),
            pltpu.VMEM((rows + 2 * width, ny), land_mask.dtype),
            pltpu.VMEM((groups * depth, rows, lev, ny), jnp.bfloat16),
            pltpu.VMEM(pert.shape, pert.dtype),
            pltpu.SemaphoreType.DMA((2 + 2 * depth + 2 * half * depth,)),
            pltpu.SemaphoreType.DMA((2 + 2 * depth + groups * depth,)),
            pltpu.SemaphoreType.DMA((5,)),
        ],
        compiler_params=pltpu.CompilerParams(
            collective_id=0, has_side_effects=True, vmem_limit_bytes=64 * 1024 * 1024
        ),
    )(owner, diffusivity, controls, land_mask, pert)
    return out[None]


def solution(mesh):
    return jax.shard_map(
        on_device,
        mesh=mesh,
        in_specs=(
            P("tm", "tile", None, None),
            P("tm", None, None, "tile", None, None),
            P(),
            P("tile", None),
            P(),
        ),
        out_specs=P("tm", None, "tile", None, None),
        check_vma=False,
    )
```

```python
import functools
import math

import jax
import jax.numpy as jnp
from jax import lax
from jax.experimental import pallas as pl
from jax.experimental.pallas import tpu as pltpu
from jax.sharding import PartitionSpec as P

MESH = pl.DeviceIdType.MESH

SWEEPS = 4


def lane_shifts(u):
    ny = u.shape[-1]
    lane = lax.broadcasted_iota(jnp.int32, u.shape, u.ndim - 1)
    fwd, back = pltpu.roll(u, 1, u.ndim - 1), pltpu.roll(u, ny - 1, u.ndim - 1)
    rolled = pltpu.roll(lane, 1, u.ndim - 1)
    moved = (rolled == lane - 1) | (rolled == lane + ny - 1)
    lower = jnp.where(moved, fwd, back)
    upper = jnp.where(moved, back, fwd)
    zero = jnp.zeros_like(u)
    return jnp.where(lane == 0, zero, lower), jnp.where(lane == ny - 1, zero, upper)


def fused_kernel(half, width, factor, owner_hbm, diff_hbm, ctrl_hbm, mask_hbm, pert_hbm,
                 out_ref, owner_ref, diff_ref, ext, mext, held, pert,
                 send_sem, recv_sem, load_sem):
    tile = lax.axis_index("tile")
    count = lax.axis_size("tile")
    me = lax.axis_index("tm")
    groups = lax.axis_size("tm")
    depth, rows, lev, ny = ctrl_hbm.shape
    wide = rows + 2 * width
    nhalo = 2 + 2 * depth
    right = lax.rem(tile + 1, count)
    left = lax.rem(tile + count - 1, count)
    zp = lax.rem(me + half, groups)
    base = me - lax.rem(me, half)
    peers = [base + lax.rem(lax.rem(me, half) + d, half) for d in range(1, half)]

    barrier = pltpu.get_barrier_semaphore()
    for dev in ((left, me), (right, me), (tile, zp)) + tuple((tile, p) for p in peers):
        pl.semaphore_signal(barrier, inc=1, device_id=dev, device_id_type=MESH)

    loads = [
        pltpu.make_async_copy(src, dst, load_sem.at[i])
        for i, (src, dst) in enumerate(
            [(ctrl_hbm, ext.at[:, pl.ds(width, rows)]), (mask_hbm, mext.at[pl.ds(width, rows)]),
             (diff_hbm, diff_ref), (owner_hbm, owner_ref), (pert_hbm, pert)]
        )
    ]
    for c in loads:
        c.start()
    pl.semaphore_wait(barrier, 2 + half)

    head, tail = pl.ds(0, width), pl.ds(rows - width, width)
    before, after = pl.ds(0, width), pl.ds(width + rows, width)
    plan = [
        (mask_hbm.at[tail], mext.at[before], right),
        (mask_hbm.at[head], mext.at[after], left),
    ]
    for k in range(depth):
        plan.append((ctrl_hbm.at[k, tail], ext.at[k, before], right))
        plan.append((ctrl_hbm.at[k, head], ext.at[k, after], left))
    halo = []
    for i, (src, dst, dev) in enumerate(plan):
        c = pltpu.make_async_remote_copy(
            src_ref=src, dst_ref=dst, send_sem=send_sem.at[i], recv_sem=recv_sem.at[i],
            device_id=(dev, me), device_id_type=MESH,
        )
        c.start()
        halo.append(c)
    for c in loads[:4]:
        c.wait()
    grow = tile * rows - width + lax.broadcasted_iota(jnp.int32, (wide, lev, ny), 0)
    inside = (grow >= 0) & (grow < count * rows)
    levels = lax.broadcasted_iota(jnp.int32, (wide, lev, ny), 1)
    sea = jnp.zeros((wide, lev, ny), jnp.float32)
    land = jnp.zeros((wide, lev, ny), jnp.float32)
    for l in range(lev):
        sea = jnp.where(levels == l, diff_ref[0, l], sea)
        land = jnp.where(levels == l, diff_ref[1, l], land)
    for c in halo[:2]:
        c.wait_recv()
    landed = jnp.broadcast_to(mext[...][:, None, :], (wide, lev, ny)) == 1
    coef = jnp.where(inside, jnp.where(landed, land, sea), 0.0)
    mid = coef[1:-1]
    cym, cyp = lane_shifts(mid)
    axm, axp = 0.5 * (mid + coef[:-2]), 0.5 * (mid + coef[2:])
    aym, ayp = 0.5 * (mid + cym), 0.5 * (mid + cyp)
    kept = inside[1:-1]

    def slot(g, k):
        return held.at[pl.ds(g * depth + k, 1)]

    def copy(g, k, dev, sem):
        return pltpu.make_async_remote_copy(
            src_ref=slot(g, k), dst_ref=slot(g, k), send_sem=send_sem.at[sem],
            recv_sem=recv_sem.at[nhalo + g * depth + k], device_id=(tile, dev), device_id_type=MESH,
        )

    def add(g, k, scale=None):
        member = owner_ref[g * depth + k]
        total = out_ref[...] + pert[member].astype(jnp.float32) * held[g * depth + k].astype(jnp.float32)[None]
        out_ref[...] = total if scale is None else total * scale

    sends = []
    for k in range(depth):
        for c in halo[2 + 2 * k:4 + 2 * k]:
            c.wait_recv()
        u = jnp.where(inside, ext[k], 0.0)
        for sweep_index in range(SWEEPS):
            lo, hi = sweep_index, wide - 2 - sweep_index
            centre = u[1:-1]
            uym, uyp = lane_shifts(centre)
            flux = axm[lo:hi] * (u[:-2] - centre)
            flux = flux + axp[lo:hi] * (u[2:] - centre)
            flux = flux + aym[lo:hi] * (uym - centre)
            flux = flux + ayp[lo:hi] * (uyp - centre)
            u = jnp.where(kept[lo:hi], centre + flux, 0.0)
        held[me * depth + k] = u.astype(held.dtype)
        for i, p in enumerate([zp] + peers):
            c = copy(me, k, p, nhalo + k * 2 * half + i)
            c.start()
            sends.append(c)

    for c in halo:
        c.wait_send()
    out_ref[...] = jnp.zeros(out_ref.shape, out_ref.dtype)
    loads[4].wait()
    for k in range(depth):
        add(me, k)
    for k in range(depth):
        copy(zp, k, zp, nhalo).wait_recv()
        for i, p in enumerate(peers):
            c = copy(zp, k, p, nhalo + k * 2 * half + half + i)
            c.start()
            sends.append(c)
        add(zp, k)
    for p in peers:
        for k in range(depth):
            copy(p, k, p, nhalo).wait_recv()
            add(p, k)
    for j, p in enumerate(peers):
        far = lax.rem(p + half, groups)
        for k in range(depth):
            copy(far, k, p, nhalo).wait_recv()
            last = j == len(peers) - 1 and k == depth - 1
            add(far, k, factor if last else None)
    for c in sends:
        c.wait_send()


def on_device(controls, perturbations, owner, land_mask, diffusivity):
    groups = lax.axis_size("tm")
    half = 4 if groups % 4 == 0 else groups // 2
    depth, rows, lev, ny = controls.shape
    width = SWEEPS
    pert = perturbations[0]
    factor = 1.0 / math.sqrt(owner.shape[0] - 1)
    vmem = pl.BlockSpec(memory_space=pltpu.VMEM)
    hbm = pl.BlockSpec(memory_space=pl.ANY)
    out = pl.pallas_call(
        functools.partial(fused_kernel, half, width, factor),
        out_shape=jax.ShapeDtypeStruct(pert.shape[1:], jnp.float32),
        in_specs=[hbm] * 5,
        out_specs=vmem,
        scratch_shapes=[
            pltpu.SMEM(owner.shape, owner.dtype),
            pltpu.SMEM(diffusivity.shape, diffusivity.dtype),
            pltpu.VMEM((depth, rows + 2 * width, lev, ny), controls.dtype),
            pltpu.VMEM((rows + 2 * width, ny), land_mask.dtype),
            pltpu.VMEM((groups * depth, rows, lev, ny), jnp.bfloat16),
            pltpu.VMEM(pert.shape, pert.dtype),
            pltpu.SemaphoreType.DMA((2 + 2 * depth + 2 * half * depth,)),
            pltpu.SemaphoreType.DMA((2 + 2 * depth + groups * depth,)),
            pltpu.SemaphoreType.DMA((5,)),
        ],
        compiler_params=pltpu.CompilerParams(
            collective_id=0, has_side_effects=True, vmem_limit_bytes=64 * 1024 * 1024
        ),
    )(owner, diffusivity, controls, land_mask, pert)
    return out[None]


def solution(mesh):
    return jax.shard_map(
        on_device,
        mesh=mesh,
        in_specs=(
            P("tm", "tile", None, None),
            P("tm", None, None, "tile", None, None),
            P(),
            P("tile", None),
            P(),
        ),
        out_specs=P("tm", None, "tile", None, None),
        check_vma=False,
    )
```

```python
import functools
import math

import jax
import jax.numpy as jnp
from jax import lax
from jax.experimental import pallas as pl
from jax.experimental.pallas import tpu as pltpu
from jax.sharding import PartitionSpec as P

MESH = pl.DeviceIdType.MESH

SWEEPS = 4


def lane_masks(shape):
    ny = shape[-1]
    lane = lax.broadcasted_iota(jnp.int32, shape, len(shape) - 1)
    rolled = pltpu.roll(lane, 1, len(shape) - 1)
    return lane, (rolled == lane - 1) | (rolled == lane + ny - 1)


def lane_shifts(u, masks):
    ny = u.shape[-1]
    lane, moved = masks[0][:u.shape[0]], masks[1][:u.shape[0]]
    fwd, back = pltpu.roll(u, 1, u.ndim - 1), pltpu.roll(u, ny - 1, u.ndim - 1)
    lower = jnp.where(moved, fwd, back)
    upper = jnp.where(moved, back, fwd)
    zero = jnp.zeros_like(u)
    return jnp.where(lane == 0, zero, lower), jnp.where(lane == ny - 1, zero, upper)


def fused_kernel(half, width, factor, owner_hbm, diff_hbm, ctrl_hbm, mask_hbm, pert_hbm,
                 out_ref, owner_ref, diff_ref, ext, mext, held, pert,
                 send_sem, recv_sem, load_sem):
    tile = lax.axis_index("tile")
    count = lax.axis_size("tile")
    me = lax.axis_index("tm")
    groups = lax.axis_size("tm")
    depth, rows, lev, ny = ctrl_hbm.shape
    wide = rows + 2 * width
    nhalo = 2 + 2 * depth
    right = lax.rem(tile + 1, count)
    left = lax.rem(tile + count - 1, count)
    zp = lax.rem(me + half, groups)
    base = me - lax.rem(me, half)
    peers = [base + lax.rem(lax.rem(me, half) + d, half) for d in range(1, half)]

    barrier = pltpu.get_barrier_semaphore()
    for dev in ((left, me), (right, me), (tile, zp)) + tuple((tile, p) for p in peers):
        pl.semaphore_signal(barrier, inc=1, device_id=dev, device_id_type=MESH)

    loads = [
        pltpu.make_async_copy(src, dst, load_sem.at[i])
        for i, (src, dst) in enumerate(
            [(ctrl_hbm, ext.at[:, pl.ds(width, rows)]), (mask_hbm, mext.at[pl.ds(width, rows)]),
             (diff_hbm, diff_ref), (owner_hbm, owner_ref), (pert_hbm, pert)]
        )
    ]
    for c in loads:
        c.start()
    pl.semaphore_wait(barrier, 2 + half)

    head, tail = pl.ds(0, width), pl.ds(rows - width, width)
    before, after = pl.ds(0, width), pl.ds(width + rows, width)
    plan = [
        (mask_hbm.at[tail], mext.at[before], right),
        (mask_hbm.at[head], mext.at[after], left),
    ]
    for k in range(depth):
        plan.append((ctrl_hbm.at[k, tail], ext.at[k, before], right))
        plan.append((ctrl_hbm.at[k, head], ext.at[k, after], left))
    halo = []
    for i, (src, dst, dev) in enumerate(plan):
        c = pltpu.make_async_remote_copy(
            src_ref=src, dst_ref=dst, send_sem=send_sem.at[i], recv_sem=recv_sem.at[i],
            device_id=(dev, me), device_id_type=MESH,
        )
        c.start()
        halo.append(c)
    for c in loads[:4]:
        c.wait()
    grow = tile * rows - width + lax.broadcasted_iota(jnp.int32, (wide, lev, ny), 0)
    inside = (grow >= 0) & (grow < count * rows)
    levels = lax.broadcasted_iota(jnp.int32, (wide, lev, ny), 1)
    sea = jnp.zeros((wide, lev, ny), jnp.float32)
    land = jnp.zeros((wide, lev, ny), jnp.float32)
    for l in range(lev):
        sea = jnp.where(levels == l, diff_ref[0, l], sea)
        land = jnp.where(levels == l, diff_ref[1, l], land)
    for c in halo[:2]:
        c.wait_recv()
    landed = jnp.broadcast_to(mext[...][:, None, :], (wide, lev, ny)) == 1
    coef = jnp.where(inside, jnp.where(landed, land, sea), 0.0)
    mid = coef[1:-1]
    masks = lane_masks(mid.shape)
    cym, cyp = lane_shifts(mid, masks)
    axm, axp = 0.5 * (mid + coef[:-2]), 0.5 * (mid + coef[2:])
    aym, ayp = 0.5 * (mid + cym), 0.5 * (mid + cyp)
    kept = inside[1:-1]

    def slot(g, k):
        return held.at[pl.ds(g * depth + k, 1)]

    def copy(g, k, dev, sem):
        return pltpu.make_async_remote_copy(
            src_ref=slot(g, k), dst_ref=slot(g, k), send_sem=send_sem.at[sem],
            recv_sem=recv_sem.at[nhalo + g * depth + k], device_id=(tile, dev), device_id_type=MESH,
        )

    def add(g, k, scale=None):
        member = owner_ref[g * depth + k]
        total = out_ref[...] + pert[member].astype(jnp.float32) * held[g * depth + k].astype(jnp.float32)[None]
        out_ref[...] = total if scale is None else total * scale

    sends = []
    for k in range(depth):
        for c in halo[2 + 2 * k:4 + 2 * k]:
            c.wait_recv()
        u = jnp.where(inside, ext[k], 0.0)
        for sweep_index in range(SWEEPS):
            lo, hi = sweep_index, wide - 2 - sweep_index
            centre = u[1:-1]
            uym, uyp = lane_shifts(centre, masks)
            flux = axm[lo:hi] * (u[:-2] - centre)
            flux = flux + axp[lo:hi] * (u[2:] - centre)
            flux = flux + aym[lo:hi] * (uym - centre)
            flux = flux + ayp[lo:hi] * (uyp - centre)
            u = jnp.where(kept[lo:hi], centre + flux, 0.0)
        held[me * depth + k] = u.astype(held.dtype)
        for i, p in enumerate([zp] + peers):
            c = copy(me, k, p, nhalo + k * 2 * half + i)
            c.start()
            sends.append(c)

    for c in halo:
        c.wait_send()
    out_ref[...] = jnp.zeros(out_ref.shape, out_ref.dtype)
    loads[4].wait()
    for k in range(depth):
        add(me, k)
    for k in range(depth):
        copy(zp, k, zp, nhalo).wait_recv()
        for i, p in enumerate(peers):
            c = copy(zp, k, p, nhalo + k * 2 * half + half + i)
            c.start()
            sends.append(c)
        add(zp, k)
    for p in peers:
        for k in range(depth):
            copy(p, k, p, nhalo).wait_recv()
            add(p, k)
    for j, p in enumerate(peers):
        far = lax.rem(p + half, groups)
        for k in range(depth):
            copy(far, k, p, nhalo).wait_recv()
            last = j == len(peers) - 1 and k == depth - 1
            add(far, k, factor if last else None)
    for c in sends:
        c.wait_send()


def on_device(controls, perturbations, owner, land_mask, diffusivity):
    groups = lax.axis_size("tm")
    half = 4 if groups % 4 == 0 else groups // 2
    depth, rows, lev, ny = controls.shape
    width = SWEEPS
    pert = perturbations[0]
    factor = 1.0 / math.sqrt(owner.shape[0] - 1)
    vmem = pl.BlockSpec(memory_space=pltpu.VMEM)
    hbm = pl.BlockSpec(memory_space=pl.ANY)
    out = pl.pallas_call(
        functools.partial(fused_kernel, half, width, factor),
        out_shape=jax.ShapeDtypeStruct(pert.shape[1:], jnp.float32),
        in_specs=[hbm] * 5,
        out_specs=vmem,
        scratch_shapes=[
            pltpu.SMEM(owner.shape, owner.dtype),
            pltpu.SMEM(diffusivity.shape, diffusivity.dtype),
            pltpu.VMEM((depth, rows + 2 * width, lev, ny), controls.dtype),
            pltpu.VMEM((rows + 2 * width, ny), land_mask.dtype),
            pltpu.VMEM((groups * depth, rows, lev, ny), jnp.bfloat16),
            pltpu.VMEM(pert.shape, pert.dtype),
            pltpu.SemaphoreType.DMA((2 + 2 * depth + 2 * half * depth,)),
            pltpu.SemaphoreType.DMA((2 + 2 * depth + groups * depth,)),
            pltpu.SemaphoreType.DMA((5,)),
        ],
        compiler_params=pltpu.CompilerParams(
            collective_id=0, has_side_effects=True, vmem_limit_bytes=64 * 1024 * 1024
        ),
    )(owner, diffusivity, controls, land_mask, pert)
    return out[None]


def solution(mesh):
    return jax.shard_map(
        on_device,
        mesh=mesh,
        in_specs=(
            P("tm", "tile", None, None),
            P("tm", None, None, "tile", None, None),
            P(),
            P("tile", None),
            P(),
        ),
        out_specs=P("tm", None, "tile", None, None),
        check_vma=False,
    )
```

```python
import functools
import math

import jax
import jax.numpy as jnp
from jax import lax
from jax.experimental import pallas as pl
from jax.experimental.pallas import tpu as pltpu
from jax.sharding import PartitionSpec as P

MESH = pl.DeviceIdType.MESH

SWEEPS = 4


def lane_shifts(u):
    ny = u.shape[-1]
    lane = lax.broadcasted_iota(jnp.int32, u.shape, u.ndim - 1)
    fwd, back = pltpu.roll(u, 1, u.ndim - 1), pltpu.roll(u, ny - 1, u.ndim - 1)
    rolled = pltpu.roll(lane, 1, u.ndim - 1)
    moved = (rolled == lane - 1) | (rolled == lane + ny - 1)
    lower = jnp.where(moved, fwd, back)
    upper = jnp.where(moved, back, fwd)
    zero = jnp.zeros_like(u)
    return jnp.where(lane == 0, zero, lower), jnp.where(lane == ny - 1, zero, upper)


def fused_kernel(half, width, factor, owner_hbm, diff_hbm, ctrl_hbm, mask_hbm, pert_hbm,
                 out_ref, owner_ref, diff_ref, ext, mext, held, pert,
                 send_sem, recv_sem, load_sem):
    tile = lax.axis_index("tile")
    count = lax.axis_size("tile")
    me = lax.axis_index("tm")
    groups = lax.axis_size("tm")
    depth, rows, lev, ny = ctrl_hbm.shape
    wide = rows + 2 * width
    nhalo = 2 + 2 * depth
    right = lax.rem(tile + 1, count)
    left = lax.rem(tile + count - 1, count)
    zp = lax.rem(me + half, groups)
    base = me - lax.rem(me, half)
    peers = [base + lax.rem(lax.rem(me, half) + d, half) for d in range(1, half)]

    barrier = pltpu.get_barrier_semaphore()
    for dev in ((left, me), (right, me), (tile, zp)) + tuple((tile, p) for p in peers):
        pl.semaphore_signal(barrier, inc=1, device_id=dev, device_id_type=MESH)

    loads = [
        pltpu.make_async_copy(src, dst, load_sem.at[i])
        for i, (src, dst) in enumerate(
            [(ctrl_hbm, ext.at[:, pl.ds(width, rows)]), (mask_hbm, mext.at[pl.ds(width, rows)]),
             (diff_hbm, diff_ref), (owner_hbm, owner_ref), (pert_hbm, pert)]
        )
    ]
    for c in loads:
        c.start()
    pl.semaphore_wait(barrier, 2 + half)

    head, tail = pl.ds(0, width), pl.ds(rows - width, width)
    before, after = pl.ds(0, width), pl.ds(width + rows, width)
    plan = [
        (mask_hbm.at[tail], mext.at[before], right),
        (mask_hbm.at[head], mext.at[after], left),
    ]
    for k in range(depth):
        plan.append((ctrl_hbm.at[k, tail], ext.at[k, before], right))
        plan.append((ctrl_hbm.at[k, head], ext.at[k, after], left))
    halo = []
    for i, (src, dst, dev) in enumerate(plan):
        c = pltpu.make_async_remote_copy(
            src_ref=src, dst_ref=dst, send_sem=send_sem.at[i], recv_sem=recv_sem.at[i],
            device_id=(dev, me), device_id_type=MESH,
        )
        c.start()
        halo.append(c)
    for c in loads[:4]:
        c.wait()
    grow = tile * rows - width + lax.broadcasted_iota(jnp.int32, (wide, lev, ny), 0)
    inside = (grow >= 0) & (grow < count * rows)
    levels = lax.broadcasted_iota(jnp.int32, (wide, lev, ny), 1)
    sea = jnp.zeros((wide, lev, ny), jnp.float32)
    land = jnp.zeros((wide, lev, ny), jnp.float32)
    for l in range(lev):
        sea = jnp.where(levels == l, diff_ref[0, l], sea)
        land = jnp.where(levels == l, diff_ref[1, l], land)
    for c in halo[:2]:
        c.wait_recv()
    landed = jnp.broadcast_to(mext[...][:, None, :], (wide, lev, ny)) == 1
    coef = jnp.where(inside, jnp.where(landed, land, sea), 0.0)
    mid = coef[1:-1]
    cym, cyp = lane_shifts(mid)
    axm, axp = 0.5 * (mid + coef[:-2]), 0.5 * (mid + coef[2:])
    aym, ayp = 0.5 * (mid + cym), 0.5 * (mid + cyp)
    kept = inside[1:-1]

    def slot(g, k):
        return held.at[pl.ds(g * depth + k, 1)]

    def copy(g, k, dev, sem):
        return pltpu.make_async_remote_copy(
            src_ref=slot(g, k), dst_ref=slot(g, k), send_sem=send_sem.at[sem],
            recv_sem=recv_sem.at[nhalo + g * depth + k], device_id=(tile, dev), device_id_type=MESH,
        )

    def add(g, k, scale=None, first=False):
        member = owner_ref[g * depth + k]
        term = pert[member].astype(jnp.float32) * held[g * depth + k].astype(jnp.float32)[None]
        total = term if first else out_ref[...] + term
        out_ref[...] = total if scale is None else total * scale

    sends = []
    for k in range(depth):
        for c in halo[2 + 2 * k:4 + 2 * k]:
            c.wait_recv()
        u = jnp.where(inside, ext[k], 0.0)
        for sweep_index in range(SWEEPS):
            lo, hi = sweep_index, wide - 2 - sweep_index
            centre = u[1:-1]
            uym, uyp = lane_shifts(centre)
            flux = axm[lo:hi] * (u[:-2] - centre)
            flux = flux + axp[lo:hi] * (u[2:] - centre)
            flux = flux + aym[lo:hi] * (uym - centre)
            flux = flux + ayp[lo:hi] * (uyp - centre)
            u = jnp.where(kept[lo:hi], centre + flux, 0.0)
        held[me * depth + k] = u.astype(held.dtype)
        for i, p in enumerate([zp] + peers):
            c = copy(me, k, p, nhalo + k * 2 * half + i)
            c.start()
            sends.append(c)

    for c in halo:
        c.wait_send()
    loads[4].wait()
    for k in range(depth):
        add(me, k, first=k == 0)
    for k in range(depth):
        copy(zp, k, zp, nhalo).wait_recv()
        for i, p in enumerate(peers):
            c = copy(zp, k, p, nhalo + k * 2 * half + half + i)
            c.start()
            sends.append(c)
        add(zp, k)
    for p in peers:
        for k in range(depth):
            copy(p, k, p, nhalo).wait_recv()
            add(p, k)
    for j, p in enumerate(peers):
        far = lax.rem(p + half, groups)
        for k in range(depth):
            copy(far, k, p, nhalo).wait_recv()
            last = j == len(peers) - 1 and k == depth - 1
            add(far, k, factor if last else None)
    for c in sends:
        c.wait_send()


def on_device(controls, perturbations, owner, land_mask, diffusivity):
    groups = lax.axis_size("tm")
    half = 4 if groups % 4 == 0 else groups // 2
    depth, rows, lev, ny = controls.shape
    width = SWEEPS
    pert = perturbations[0]
    factor = 1.0 / math.sqrt(owner.shape[0] - 1)
    vmem = pl.BlockSpec(memory_space=pltpu.VMEM)
    hbm = pl.BlockSpec(memory_space=pl.ANY)
    out = pl.pallas_call(
        functools.partial(fused_kernel, half, width, factor),
        out_shape=jax.ShapeDtypeStruct(pert.shape[1:], jnp.float32),
        in_specs=[hbm] * 5,
        out_specs=vmem,
        scratch_shapes=[
            pltpu.SMEM(owner.shape, owner.dtype),
            pltpu.SMEM(diffusivity.shape, diffusivity.dtype),
            pltpu.VMEM((depth, rows + 2 * width, lev, ny), controls.dtype),
            pltpu.VMEM((rows + 2 * width, ny), land_mask.dtype),
            pltpu.VMEM((groups * depth, rows, lev, ny), jnp.bfloat16),
            pltpu.VMEM(pert.shape, pert.dtype),
            pltpu.SemaphoreType.DMA((2 + 2 * depth + 2 * half * depth,)),
            pltpu.SemaphoreType.DMA((2 + 2 * depth + groups * depth,)),
            pltpu.SemaphoreType.DMA((5,)),
        ],
        compiler_params=pltpu.CompilerParams(
            collective_id=0, has_side_effects=True, vmem_limit_bytes=64 * 1024 * 1024
        ),
    )(owner, diffusivity, controls, land_mask, pert)
    return out[None]


def solution(mesh):
    return jax.shard_map(
        on_device,
        mesh=mesh,
        in_specs=(
            P("tm", "tile", None, None),
            P("tm", None, None, "tile", None, None),
            P(),
            P("tile", None),
            P(),
        ),
        out_specs=P("tm", None, "tile", None, None),
        check_vma=False,
    )
```

```python
import functools
import math

import jax
import jax.numpy as jnp
from jax import lax
from jax.experimental import pallas as pl
from jax.experimental.pallas import tpu as pltpu
from jax.sharding import PartitionSpec as P

MESH = pl.DeviceIdType.MESH

SWEEPS = 4


def lane_shifts(u):
    ny = u.shape[-1]
    lane = lax.broadcasted_iota(jnp.int32, u.shape, u.ndim - 1)
    fwd, back = pltpu.roll(u, 1, u.ndim - 1), pltpu.roll(u, ny - 1, u.ndim - 1)
    rolled = pltpu.roll(lane, 1, u.ndim - 1)
    moved = (rolled == lane - 1) | (rolled == lane + ny - 1)
    lower = jnp.where(moved, fwd, back)
    upper = jnp.where(moved, back, fwd)
    zero = jnp.zeros_like(u)
    return jnp.where(lane == 0, zero, lower), jnp.where(lane == ny - 1, zero, upper)


def fused_kernel(half, width, factor, owner_hbm, diff_hbm, ctrl_hbm, mask_hbm, pert_hbm,
                 out_ref, owner_ref, diff_ref, ext, mext, held, pert,
                 send_sem, recv_sem, load_sem):
    tile = lax.axis_index("tile")
    count = lax.axis_size("tile")
    me = lax.axis_index("tm")
    groups = lax.axis_size("tm")
    depth, rows, lev, ny = ctrl_hbm.shape
    wide = rows + 2 * width
    nhalo = 2 + 2 * depth
    right = lax.rem(tile + 1, count)
    left = lax.rem(tile + count - 1, count)
    zp = lax.rem(me + half, groups)
    base = me - lax.rem(me, half)
    peers = [base + lax.rem(lax.rem(me, half) + d, half) for d in range(1, half)]

    barrier = pltpu.get_barrier_semaphore()
    for dev in ((left, me), (right, me), (tile, zp)) + tuple((tile, p) for p in peers):
        pl.semaphore_signal(barrier, inc=1, device_id=dev, device_id_type=MESH)

    loads = [
        pltpu.make_async_copy(src, dst, load_sem.at[i])
        for i, (src, dst) in enumerate(
            [(ctrl_hbm, ext.at[:, pl.ds(width, rows)]), (mask_hbm, mext.at[pl.ds(width, rows)]),
             (diff_hbm, diff_ref), (owner_hbm, owner_ref), (pert_hbm, pert)]
        )
    ]
    for c in loads:
        c.start()
    pl.semaphore_wait(barrier, 2 + half)

    head, tail = pl.ds(0, width), pl.ds(rows - width, width)
    before, after = pl.ds(0, width), pl.ds(width + rows, width)
    plan = [
        (mask_hbm.at[tail], mext.at[before], right),
        (mask_hbm.at[head], mext.at[after], left),
    ]
    for k in range(depth):
        plan.append((ctrl_hbm.at[k, tail], ext.at[k, before], right))
        plan.append((ctrl_hbm.at[k, head], ext.at[k, after], left))
    halo = []
    for i, (src, dst, dev) in enumerate(plan):
        c = pltpu.make_async_remote_copy(
            src_ref=src, dst_ref=dst, send_sem=send_sem.at[i], recv_sem=recv_sem.at[i],
            device_id=(dev, me), device_id_type=MESH,
        )
        c.start()
        halo.append(c)
    for c in loads[:4]:
        c.wait()
    grow = tile * rows - width + lax.broadcasted_iota(jnp.int32, (wide, lev, ny), 0)
    inside = (grow >= 0) & (grow < count * rows)
    levels = lax.broadcasted_iota(jnp.int32, (wide, lev, ny), 1)
    sea = jnp.zeros((wide, lev, ny), jnp.float32)
    land = jnp.zeros((wide, lev, ny), jnp.float32)
    for l in range(lev):
        sea = jnp.where(levels == l, diff_ref[0, l], sea)
        land = jnp.where(levels == l, diff_ref[1, l], land)
    for c in halo[:2]:
        c.wait_recv()
    landed = jnp.broadcast_to(mext[...][:, None, :], (wide, lev, ny)) == 1
    coef = jnp.where(inside, jnp.where(landed, land, sea), 0.0)
    mid = coef[1:-1]
    cym, cyp = lane_shifts(mid)
    axm, axp = 0.5 * (mid + coef[:-2]), 0.5 * (mid + coef[2:])
    aym, ayp = 0.5 * (mid + cym), 0.5 * (mid + cyp)
    kept = inside[1:-1]

    def slot(g, k):
        return held.at[pl.ds(g * depth + k, 1)]

    def copy(g, k, dev, sem):
        return pltpu.make_async_remote_copy(
            src_ref=slot(g, k), dst_ref=slot(g, k), send_sem=send_sem.at[sem],
            recv_sem=recv_sem.at[nhalo + g * depth + k], device_id=(tile, dev), device_id_type=MESH,
        )

    def add(g, k, scale=None):
        member = owner_ref[g * depth + k]
        total = out_ref[...] + pert[member].astype(jnp.float32) * held[g * depth + k].astype(jnp.float32)[None]
        out_ref[...] = total if scale is None else total * scale

    sends = []
    for k in range(depth):
        for c in halo[2 + 2 * k:4 + 2 * k]:
            c.wait_recv()
        u = jnp.where(inside, ext[k], 0.0)
        for sweep_index in range(SWEEPS):
            lo, hi = sweep_index, wide - 2 - sweep_index
            centre = u[1:-1]
            uym, uyp = lane_shifts(centre)
            flux = axm[lo:hi] * (u[:-2] - centre)
            flux = flux + axp[lo:hi] * (u[2:] - centre)
            flux = flux + aym[lo:hi] * (uym - centre)
            flux = flux + ayp[lo:hi] * (uyp - centre)
            u = jnp.where(kept[lo:hi], centre + flux, 0.0)
        held[me * depth + k] = u.astype(held.dtype)
        for i, p in enumerate([zp] + peers):
            c = copy(me, k, p, nhalo + k * 2 * half + i)
            c.start()
            sends.append(c)

    for c in halo:
        c.wait_send()
    out_ref[...] = jnp.zeros(out_ref.shape, out_ref.dtype)
    loads[4].wait()
    for k in range(depth):
        add(me, k)
    for k in range(depth):
        copy(zp, k, zp, nhalo).wait_recv()
        for i, p in enumerate(peers):
            c = copy(zp, k, p, nhalo + k * 2 * half + half + i)
            c.start()
            sends.append(c)
    for k in range(depth):
        add(zp, k)
    for p in peers:
        for k in range(depth):
            copy(p, k, p, nhalo).wait_recv()
            add(p, k)
    for j, p in enumerate(peers):
        far = lax.rem(p + half, groups)
        for k in range(depth):
            copy(far, k, p, nhalo).wait_recv()
            last = j == len(peers) - 1 and k == depth - 1
            add(far, k, factor if last else None)
    for c in sends:
        c.wait_send()


def on_device(controls, perturbations, owner, land_mask, diffusivity):
    groups = lax.axis_size("tm")
    half = 4 if groups % 4 == 0 else groups // 2
    depth, rows, lev, ny = controls.shape
    width = SWEEPS
    pert = perturbations[0]
    factor = 1.0 / math.sqrt(owner.shape[0] - 1)
    vmem = pl.BlockSpec(memory_space=pltpu.VMEM)
    hbm = pl.BlockSpec(memory_space=pl.ANY)
    out = pl.pallas_call(
        functools.partial(fused_kernel, half, width, factor),
        out_shape=jax.ShapeDtypeStruct(pert.shape[1:], jnp.float32),
        in_specs=[hbm] * 5,
        out_specs=vmem,
        scratch_shapes=[
            pltpu.SMEM(owner.shape, owner.dtype),
            pltpu.SMEM(diffusivity.shape, diffusivity.dtype),
            pltpu.VMEM((depth, rows + 2 * width, lev, ny), controls.dtype),
            pltpu.VMEM((rows + 2 * width, ny), land_mask.dtype),
            pltpu.VMEM((groups * depth, rows, lev, ny), jnp.bfloat16),
            pltpu.VMEM(pert.shape, pert.dtype),
            pltpu.SemaphoreType.DMA((2 + 2 * depth + 2 * half * depth,)),
            pltpu.SemaphoreType.DMA((2 + 2 * depth + groups * depth,)),
            pltpu.SemaphoreType.DMA((5,)),
        ],
        compiler_params=pltpu.CompilerParams(
            collective_id=0, has_side_effects=True, vmem_limit_bytes=64 * 1024 * 1024
        ),
    )(owner, diffusivity, controls, land_mask, pert)
    return out[None]


def solution(mesh):
    return jax.shard_map(
        on_device,
        mesh=mesh,
        in_specs=(
            P("tm", "tile", None, None),
            P("tm", None, None, "tile", None, None),
            P(),
            P("tile", None),
            P(),
        ),
        out_specs=P("tm", None, "tile", None, None),
        check_vma=False,
    )
```

```python
import functools
import math

import jax
import jax.numpy as jnp
from jax import lax
from jax.experimental import pallas as pl
from jax.experimental.pallas import tpu as pltpu
from jax.sharding import PartitionSpec as P

MESH = pl.DeviceIdType.MESH

SWEEPS = 4


def lane_shifts(u):
    ny = u.shape[-1]
    lane = lax.broadcasted_iota(jnp.int32, u.shape, u.ndim - 1)
    fwd, back = pltpu.roll(u, 1, u.ndim - 1), pltpu.roll(u, ny - 1, u.ndim - 1)
    rolled = pltpu.roll(lane, 1, u.ndim - 1)
    moved = (rolled == lane - 1) | (rolled == lane + ny - 1)
    lower = jnp.where(moved, fwd, back)
    upper = jnp.where(moved, back, fwd)
    zero = jnp.zeros_like(u)
    return jnp.where(lane == 0, zero, lower), jnp.where(lane == ny - 1, zero, upper)


def fused_kernel(half, width, factor, owner_hbm, diff_hbm, ctrl_hbm, mask_hbm, pert_hbm,
                 out_ref, owner_ref, diff_ref, ext, mext, held, pert,
                 send_sem, recv_sem, load_sem):
    tile = lax.axis_index("tile")
    count = lax.axis_size("tile")
    me = lax.axis_index("tm")
    groups = lax.axis_size("tm")
    depth, rows, lev, ny = ctrl_hbm.shape
    wide = rows + 2 * width
    nhalo = 2 + 2 * depth
    right = lax.rem(tile + 1, count)
    left = lax.rem(tile + count - 1, count)
    zp = lax.rem(me + half, groups)
    base = me - lax.rem(me, half)
    peers = [base + lax.rem(lax.rem(me, half) + d, half) for d in range(1, half)]

    barrier = pltpu.get_barrier_semaphore()
    for dev in ((tile, zp), (left, me), (right, me)) + tuple((tile, p) for p in peers):
        pl.semaphore_signal(barrier, inc=1, device_id=dev, device_id_type=MESH)

    loads = [
        pltpu.make_async_copy(src, dst, load_sem.at[i])
        for i, (src, dst) in enumerate(
            [(ctrl_hbm, ext.at[:, pl.ds(width, rows)]), (mask_hbm, mext.at[pl.ds(width, rows)]),
             (diff_hbm, diff_ref), (owner_hbm, owner_ref), (pert_hbm, pert)]
        )
    ]
    for c in loads:
        c.start()
    pl.semaphore_wait(barrier, 2 + half)

    head, tail = pl.ds(0, width), pl.ds(rows - width, width)
    before, after = pl.ds(0, width), pl.ds(width + rows, width)
    plan = [
        (mask_hbm.at[tail], mext.at[before], right),
        (mask_hbm.at[head], mext.at[after], left),
    ]
    for k in range(depth):
        plan.append((ctrl_hbm.at[k, tail], ext.at[k, before], right))
        plan.append((ctrl_hbm.at[k, head], ext.at[k, after], left))
    halo = []
    for i, (src, dst, dev) in enumerate(plan):
        c = pltpu.make_async_remote_copy(
            src_ref=src, dst_ref=dst, send_sem=send_sem.at[i], recv_sem=recv_sem.at[i],
            device_id=(dev, me), device_id_type=MESH,
        )
        c.start()
        halo.append(c)
    for c in loads[:4]:
        c.wait()
    grow = tile * rows - width + lax.broadcasted_iota(jnp.int32, (wide, lev, ny), 0)
    inside = (grow >= 0) & (grow < count * rows)
    levels = lax.broadcasted_iota(jnp.int32, (wide, lev, ny), 1)
    sea = jnp.zeros((wide, lev, ny), jnp.float32)
    land = jnp.zeros((wide, lev, ny), jnp.float32)
    for l in range(lev):
        sea = jnp.where(levels == l, diff_ref[0, l], sea)
        land = jnp.where(levels == l, diff_ref[1, l], land)
    for c in halo[:2]:
        c.wait_recv()
    landed = jnp.broadcast_to(mext[...][:, None, :], (wide, lev, ny)) == 1
    coef = jnp.where(inside, jnp.where(landed, land, sea), 0.0)
    mid = coef[1:-1]
    cym, cyp = lane_shifts(mid)
    axm, axp = 0.5 * (mid + coef[:-2]), 0.5 * (mid + coef[2:])
    aym, ayp = 0.5 * (mid + cym), 0.5 * (mid + cyp)
    kept = inside[1:-1]

    def slot(g, k):
        return held.at[pl.ds(g * depth + k, 1)]

    def copy(g, k, dev, sem):
        return pltpu.make_async_remote_copy(
            src_ref=slot(g, k), dst_ref=slot(g, k), send_sem=send_sem.at[sem],
            recv_sem=recv_sem.at[nhalo + g * depth + k], device_id=(tile, dev), device_id_type=MESH,
        )

    def add(g, k, scale=None):
        member = owner_ref[g * depth + k]
        total = out_ref[...] + pert[member].astype(jnp.float32) * held[g * depth + k].astype(jnp.float32)[None]
        out_ref[...] = total if scale is None else total * scale

    sends = []
    for k in range(depth):
        for c in halo[2 + 2 * k:4 + 2 * k]:
            c.wait_recv()
        u = jnp.where(inside, ext[k], 0.0)
        for sweep_index in range(SWEEPS):
            lo, hi = sweep_index, wide - 2 - sweep_index
            centre = u[1:-1]
            uym, uyp = lane_shifts(centre)
            flux = axm[lo:hi] * (u[:-2] - centre)
            flux = flux + axp[lo:hi] * (u[2:] - centre)
            flux = flux + aym[lo:hi] * (uym - centre)
            flux = flux + ayp[lo:hi] * (uyp - centre)
            u = jnp.where(kept[lo:hi], centre + flux, 0.0)
        held[me * depth + k] = u.astype(held.dtype)
        for i, p in enumerate([zp] + peers):
            c = copy(me, k, p, nhalo + k * 2 * half + i)
            c.start()
            sends.append(c)

    for c in halo:
        c.wait_send()
    out_ref[...] = jnp.zeros(out_ref.shape, out_ref.dtype)
    loads[4].wait()
    for k in range(depth):
        add(me, k)
    for k in range(depth):
        copy(zp, k, zp, nhalo).wait_recv()
        for i, p in enumerate(peers):
            c = copy(zp, k, p, nhalo + k * 2 * half + half + i)
            c.start()
            sends.append(c)
        add(zp, k)
    for p in peers:
        for k in range(depth):
            copy(p, k, p, nhalo).wait_recv()
            add(p, k)
    for j, p in enumerate(peers):
        far = lax.rem(p + half, groups)
        for k in range(depth):
            copy(far, k, p, nhalo).wait_recv()
            last = j == len(peers) - 1 and k == depth - 1
            add(far, k, factor if last else None)
    for c in sends:
        c.wait_send()


def on_device(controls, perturbations, owner, land_mask, diffusivity):
    groups = lax.axis_size("tm")
    half = 4 if groups % 4 == 0 else groups // 2
    depth, rows, lev, ny = controls.shape
    width = SWEEPS
    pert = perturbations[0]
    factor = 1.0 / math.sqrt(owner.shape[0] - 1)
    vmem = pl.BlockSpec(memory_space=pltpu.VMEM)
    hbm = pl.BlockSpec(memory_space=pl.ANY)
    out = pl.pallas_call(
        functools.partial(fused_kernel, half, width, factor),
        out_shape=jax.ShapeDtypeStruct(pert.shape[1:], jnp.float32),
        in_specs=[hbm] * 5,
        out_specs=vmem,
        scratch_shapes=[
            pltpu.SMEM(owner.shape, owner.dtype),
            pltpu.SMEM(diffusivity.shape, diffusivity.dtype),
            pltpu.VMEM((depth, rows + 2 * width, lev, ny), controls.dtype),
            pltpu.VMEM((rows + 2 * width, ny), land_mask.dtype),
            pltpu.VMEM((groups * depth, rows, lev, ny), jnp.bfloat16),
            pltpu.VMEM(pert.shape, pert.dtype),
            pltpu.SemaphoreType.DMA((2 + 2 * depth + 2 * half * depth,)),
            pltpu.SemaphoreType.DMA((2 + 2 * depth + groups * depth,)),
            pltpu.SemaphoreType.DMA((5,)),
        ],
        compiler_params=pltpu.CompilerParams(
            collective_id=0, has_side_effects=True, vmem_limit_bytes=64 * 1024 * 1024
        ),
    )(owner, diffusivity, controls, land_mask, pert)
    return out[None]


def solution(mesh):
    return jax.shard_map(
        on_device,
        mesh=mesh,
        in_specs=(
            P("tm", "tile", None, None),
            P("tm", None, None, "tile", None, None),
            P(),
            P("tile", None),
            P(),
        ),
        out_specs=P("tm", None, "tile", None, None),
        check_vma=False,
    )
```
